32 devices in a mesh: wide: 2 (over x), grow: 4 (over y, core), gcol: 4 (over z).
Axes of the slice: x: 2, y: 2, z: 4, core: 2. Of those that a mesh axis runs over, the one named last changes fastest.
Arguments:
- diag_block: float32 [2, 1024, 1024], P('wide', ('grow', 'gcol')), as said below
- lower_block: float32 [2, 3072, 1024], P('wide', ('grow', 'gcol')), may hold values from -0.1875 to 0.1875
- trailing_block: float32 [2, 3072, 3072], P('wide', 'grow', 'gcol'), as said below
- parent_front: float32 [4, 2048, 8192], P('grow', 'wide', 'gcol'), may hold values from -3 to 3
- row_map: int32 [2, 24], replicated, may hold values from 0 to 63, as said below
Outputs:
- factor: float32 [2, 1024, 1024], P('wide', ('grow', 'gcol'))
- panel: float32 [2, 3072, 1024], P('wide', ('grow', 'gcol'))
- parent: float32 [4, 2048, 8192], P('grow', 'wide', 'gcol')
The draws below stay inside these ranges and needn't reach their ends.
Inputs may be any that keep to these rules, and one draw needn't show every extreme that they name: Each diag_block[g] is symmetric and positive definite. Each trailing_block[g] is symmetric. `row_map`: the blocks of one child are distinct, and child block b goes to a grandparent block p with p // 16 equal to b // 6.
All inputs are finite; a program needn't handle non-finite values.
Results may differ from the reference program's by a relative error of at most 0.0003.
Values sent between devices are 32-bit elements; how exact they have to be, the bound alone decides.
A program may use at most 128 MiB of HBM per device.

```python
import jax
import jax.numpy as jnp
from jax import lax

NS = 1024
NC = 3072
PN = 8192
BLOCK = 128
GROUPS = 2
QUARTERS = 4
PQ = 2048


def draw_diag_block(key, part):
    noise = jax.random.normal(key, (GROUPS, NS, NS), jnp.float32)
    sym = (noise + jnp.swapaxes(noise, 1, 2)) * (0.5 / NS ** 0.5)
    base = 2.5 + jax.random.uniform(jax.random.fold_in(key, 1), (GROUPS, NS), jnp.float32, 0.0, 1.5)
    matrix = sym + base[:, :, None] * jnp.eye(NS, dtype=jnp.float32)[None]
    return matrix


def draw_trailing_block(key, part):
    noise = jax.random.normal(key, (GROUPS, NC, NC), jnp.float32)
    sym = (noise + jnp.swapaxes(noise, 1, 2)) * (0.5 / NC ** 0.5)
    base = jax.random.uniform(jax.random.fold_in(key, 1), (GROUPS, NC), jnp.float32, 0.5, 1.5)
    return sym + base[:, :, None] * jnp.eye(NC, dtype=jnp.float32)[None]


def draw_row_map(key, part):
    quarter_blocks = PN // (BLOCK * QUARTERS)
    child_blocks = NC // (BLOCK * QUARTERS)
    keys = jax.random.split(jax.random.fold_in(key, 7), GROUPS * QUARTERS)
    orders = jax.vmap(lambda single: jax.random.permutation(single, quarter_blocks))(keys)
    picked = orders[:, :child_blocks].reshape(GROUPS, QUARTERS, child_blocks)
    shifted = picked + (jnp.arange(QUARTERS, dtype=jnp.int32) * quarter_blocks)[None, :, None]
    return shifted.reshape(GROUPS, QUARTERS * child_blocks).astype(jnp.int32)


def levels(rng, dims, cuts, least, largest):
    level = 1.0
    for dim, parts in cuts:
        steps = jax.random.uniform(jax.random.fold_in(jax.random.fold_in(rng, 6), dim), (parts,), jnp.float32, least / len(cuts), largest / len(cuts))
        level = level * jnp.repeat(jnp.exp(steps), dims[dim] // parts).reshape((-1,) + (1,) * (len(dims) - 1 - dim))
    return level


def gaussian(own_key, shape, width, reach, shards=(), kind=jnp.bfloat16):
    factor_of = levels(own_key, shape, shards, -0.22, 0.18) if shards else 1.0
    values = jax.random.normal(own_key, shape, jnp.float32) * width * factor_of
    return jnp.minimum(jnp.maximum(values, -reach), reach).astype(kind)


def setup_inputs(seed: int = 0) -> dict:
    arg_keys = jax.random.split(jax.random.key(seed), 6)
    diag_block = draw_diag_block(jax.random.fold_in(arg_keys[5], 71), 0)
    lower_block = gaussian(arg_keys[1], (GROUPS, NC, NS), NS ** -0.5, 0.1875, ((0, 2), (1, 16)), jnp.float32)
    trailing_block = draw_trailing_block(jax.random.fold_in(arg_keys[5], 71), 0)
    parent_front = gaussian(arg_keys[3], (QUARTERS, PQ, PN), 0.5, 3.0, ((0, 4), (1, 2), (2, 4)), jnp.float32)
    row_map = draw_row_map(jax.random.fold_in(arg_keys[5], 71), 0)
    return {"diag_block": diag_block, "lower_block": lower_block, "trailing_block": trailing_block, "parent_front": parent_front, "row_map": row_map}


def reference(diag_block, lower_block, trailing_block, parent_front, row_map):
    factor = jnp.linalg.cholesky(diag_block)
    solved = jax.scipy.linalg.solve_triangular(factor, jnp.swapaxes(lower_block, 1, 2), lower=True)
    panel = jnp.swapaxes(solved, 1, 2)
    schur = trailing_block - jnp.einsum('gik,gjk->gij', panel, panel, precision=lax.Precision.HIGHEST)
    order = parent_front.shape[0] * parent_front.shape[1]
    offsets = jnp.arange(BLOCK, dtype=jnp.int32)

    def add_child(total, item):
        contribution, blocks = item
        index = (blocks.astype(jnp.int32)[:, None] * BLOCK + offsets[None, :]).reshape(-1)
        return (total.at[index[:, None], index[None, :]].add(contribution), None)
    total, _ = lax.scan(add_child, parent_front.reshape(order, order), (schur, row_map))
    return (factor, panel, total.reshape(parent_front.shape))
```

```python
import functools

import jax
import jax.numpy as jnp
from jax import lax
from jax.experimental import pallas as pl
from jax.experimental.pallas import tpu as pltpu
from jax.sharding import PartitionSpec as P

BLOCK = 128
HALF = 64
F32 = jnp.float32
BF16 = jnp.bfloat16
NT = (((1,), (1,)), ((), ()))
NN = (((1,), (0,)), ((), ()))
VMEM = pl.BlockSpec(memory_space=pltpu.VMEM)
SMEM = pl.BlockSpec(memory_space=pltpu.SMEM)


def full_dot(a, b, dims):
    return lax.dot_general(
        a, b, dims, precision=lax.Precision.HIGHEST, preferred_element_type=F32
    )


def parts(x):
    high = x.astype(BF16)
    return high, (x - high.astype(F32)).astype(BF16)


def split_dot(a, b, dims):
    one = functools.partial(lax.dot_general, dimension_numbers=dims, preferred_element_type=F32)
    return one(a[0], b[0]) + (one(a[0], b[1]) + one(a[1], b[0]))


def factor_half(block):
    half = block.shape[0]
    rows = lax.broadcasted_iota(jnp.int32, (half, half), 0)
    cols = lax.broadcasted_iota(jnp.int32, (half, half), 1)
    eye = jnp.where(rows == cols, 1.0, 0.0).astype(F32)
    full = jnp.concatenate([block, eye], axis=1)
    count = half // 8
    wide = (8, 2 * half)
    groups = [full[8 * s : 8 * s + 8] for s in range(count)]
    sub = lax.broadcasted_iota(jnp.int32, wide, 0)
    done = []
    for s in range(count):
        c = 8 * s
        spread = lambda x: jnp.broadcast_to(x, wide)
        lead = [spread(groups[s][i : i + 1, :]) for i in range(8)]
        pivot = {
            (i, j): spread(lead[i][:, c + j : c + j + 1]) for i in range(8) for j in range(i, 8)
        }
        below = range(s + 1, count)
        column = {t: [spread(groups[t][:, c + j : c + j + 1]) for j in range(8)] for t in below}
        keep = jnp.zeros(wide, F32)
        for j in range(8):
            r = lax.rsqrt(pivot[j, j])
            unit = lead[j] * r
            mult = {i: pivot[j, i] * r for i in range(j + 1, 8)}
            for i in range(j + 1, 8):
                for q in range(i, 8):
                    pivot[i, q] = pivot[i, q] - mult[i] * mult[q]
                lead[i] = lead[i] - mult[i] * unit
            for t in below:
                m = column[t][j] * r
                for i in range(j + 1, 8):
                    column[t][i] = column[t][i] - m * mult[i]
                groups[t] = groups[t] - m * unit
            keep = jnp.where(sub == j, unit, keep)
        done.append(keep)
    both = jnp.concatenate(done, axis=0)
    upper = jnp.where(rows <= cols, both[:, :half], 0.0)
    inverse = jnp.where(rows >= cols, both[:, half:], 0.0)
    return upper.T, inverse


def square(a, b, c):
    return jnp.concatenate(
        [
            jnp.concatenate([a, jnp.zeros_like(a)], axis=1),
            jnp.concatenate([b, c], axis=1),
        ],
        axis=0,
    )


def factor_in_place(a, w, between):
    n = a.shape[0]
    count = n // BLOCK

    def step(k, carry):
        o = pl.multiple_of(k * BLOCK, BLOCK)
        d = a[pl.ds(o, BLOCK), pl.ds(o, BLOCK)]
        l1, w1 = factor_half(d[:HALF, :HALF])
        l21 = full_dot(d[HALF:, :HALF], w1, NT)
        l2, w2 = factor_half(d[HALF:, HALF:] - full_dot(l21, l21, NT))
        w21 = -full_dot(w2, full_dot(l21, w1, NN), NN)
        a[pl.ds(o, BLOCK), pl.ds(o, BLOCK)] = square(l1, l21, l2)
        w[k] = square(w1, w21, w2)
        for at in range(count - 1):

            @pl.when(k == at)
            def _(at=at):
                low, high = at * BLOCK, at * BLOCK + BLOCK
                a[low:high, high:] = jnp.zeros((BLOCK, n - high), F32)
                p = full_dot(a[high:, low:high], w[at], NT)
                a[high:, low:high] = p
                for c in range(high, n, 2 * BLOCK):
                    e = min(c + 2 * BLOCK, n)
                    a[c:, c:e] = a[c:, c:e] - full_dot(p[c - high :], p[c - high : e - high], NT)
                for act in between.get(at, ()):
                    act()

        return carry

    lax.fori_loop(0, count, step, 0)


def most_slots(blocks, per_owner):
    return min(blocks, per_owner)


def solve_sides(l_ref, w_ref, br_ref, bc_ref, xh, xl, lh, ll):
    n = l_ref.shape[0]
    blocks = br_ref.shape[0] // BLOCK
    few = 2
    tile = few * BLOCK
    sides = (br_ref, bc_ref)
    lh[...], ll[...] = parts(l_ref[...])
    pair = 2 * BLOCK
    for k in range(n // pair):
        low, high = k * pair, k * pair + pair
        wa, wb = w_ref[2 * k], w_ref[2 * k + 1]
        across = l_ref[low + BLOCK : high, low : low + BLOCK]
        wk = parts(square(wa, -full_dot(wb, full_dot(across, wa, NN), NN), wb))

        def solve(i, carry, low=low, high=high, wk=wk):
            o = pl.multiple_of(i * tile, tile)
            for side, b in enumerate(sides):
                rest = b[pl.ds(o, tile), low:high]
                at = pl.ds(side * blocks + i * few, few)
                if low:
                    left = tuple(x[at, :, :low].reshape(tile, low) for x in (xh, xl))
                    rest = rest - split_dot(left, (lh[low:high, :low], ll[low:high, :low]), NT)
                x = split_dot(parts(rest), wk, NT)
                for ref, value in zip((xh, xl), parts(x)):
                    ref[at, :, low:high] = value.reshape(few, BLOCK, pair)
                if side == 0:
                    br_ref[pl.ds(o, tile), low:high] = x
            return carry

        lax.fori_loop(0, blocks // few, solve, 0)


def front_kernel(
    rows, columns, owners, sure, quarter, map_ref, d_ref, x_ref, t_ref,
    factor_ref, panel_ref, piece_ref, need_ref,
    a, w, br, bc, xh, xl, lh, ll, t, stage, x_send, x_recv,
    local, line_send, line_recv, far_send, far_recv, near_send, near_recv,
    b_send, b_recv, c_send, c_recv,
):
    child = lax.axis_index("wide")
    row, column = lax.axis_index("grow"), lax.axis_index("gcol")
    q = br.shape[0]
    blocks = q // BLOCK
    per_owner = quarter // owners
    far_row = lax.rem(row + rows // 2, rows)
    near_row = row + 1 - 2 * lax.rem(row, 2)
    right, left = {"gcol": column + 1}, {"gcol": column - 1}
    far, near = {"grow": far_row}, {"grow": near_row}
    share, part = d_ref.shape[0], x_ref.shape[0]
    has_left, has_right = column > 0, column < columns - 1

    def band(r, c):
        return a.at[pl.ds(pl.multiple_of((r * columns + c) * share, share), share)]

    def piece(ref, c):
        return ref.at[pl.ds(pl.multiple_of(c * part, part), part)]

    def remote(ref, send, recv, to):
        return pltpu.make_async_remote_copy(
            src_ref=ref, dst_ref=ref, send_sem=send, recv_sem=recv,
            device_id=to, device_id_type=pl.DeviceIdType.MESH,
        )

    own_d = pltpu.make_async_copy(d_ref, band(row, column), local.at[0])
    own_x = pltpu.make_async_copy(x_ref, piece(br, column), local.at[1])
    own_t = pltpu.make_async_copy(t_ref, t, local.at[2])
    own_d.start()
    own_x.start()
    own_t.start()
    barrier = pltpu.get_barrier_semaphore()
    next_column = {"gcol": lax.rem(column + 1, columns)}
    last_column = {"gcol": lax.rem(column + columns - 1, columns)}
    for to in (far, near, next_column, last_column):
        pl.semaphore_signal(barrier, inc=1, device_id=to, device_id_type=pl.DeviceIdType.MESH)
    for d in range(1, owners):
        pl.semaphore_signal(
            barrier, inc=1, device_id={"wide": lax.rem(child + d, owners)},
            device_id_type=pl.DeviceIdType.MESH,
        )
    pl.semaphore_wait(barrier, 3 + owners)
    own_d.wait()
    own_x.wait()

    def pass_on(ref, send, recv, c, both=False):
        @pl.when((c <= column) & has_right)
        def _():
            remote(ref, send.at[0, c], recv.at[c], right).start()

        @pl.when((c >= column) & has_left)
        def _():
            remote(ref, send.at[1, c], recv.at[c], left).start()

    def passed(ref, send, recv, c):
        @pl.when((c <= column) & has_right)
        def _():
            remote(ref, send.at[0, c], recv.at[c], right).wait_send()

        @pl.when((c >= column) & has_left)
        def _():
            remote(ref, send.at[1, c], recv.at[c], left).wait_send()

    def at_distance(d, act):
        for c, there in ((column - d, column - d >= 0), (column + d, column + d < columns)):
            pl.when(there)(functools.partial(act, c))

    def spread(c):
        remote(band(row, c), far_send.at[c], far_recv.at[c], far).start()
        remote(band(row, c), near_send.at[0, c], near_recv.at[0, c], near).start()

    pass_on(band(row, column), line_send, line_recv, column)
    spread(column)

    def arrived(c):
        remote(band(row, c), line_send.at[0, c], line_recv.at[c], right).wait_recv()
        pass_on(band(row, c), line_send, line_recv, c)
        spread(c)

    def crossed(c):
        remote(band(far_row, c), far_send.at[c], far_recv.at[c], far).wait_recv()
        remote(band(far_row, c), near_send.at[1, c], near_recv.at[1, c], near).start()

    at_distance(1, arrived)
    crossed(column)
    for d in range(2, columns):
        at_distance(d, arrived)
        at_distance(d - 1, crossed)
    pass_on(piece(br, column), b_send, b_recv, column)
    at_distance(columns - 1, crossed)
    near_far_row = lax.rem(near_row + rows // 2, rows)
    for c in range(columns):
        remote(band(near_row, c), near_send.at[0, c], near_recv.at[0, c], near).wait_recv()
        remote(band(near_far_row, c), near_send.at[1, c], near_recv.at[1, c], near).wait_recv()
    for c in range(columns):
        remote(band(row, c), far_send.at[c], far_recv.at[c], far).wait_send()
        remote(band(row, c), near_send.at[0, c], near_recv.at[0, c], near).wait_send()
        remote(band(far_row, c), near_send.at[1, c], near_recv.at[1, c], near).wait_send()
        passed(band(row, c), line_send, line_recv, c)

    root = row == column
    relay = far_row == column
    from_far = relay
    from_near = jnp.logical_not(root | relay)

    def give(c):
        @pl.when(root)
        def _():
            for slot, to in ((0, far), (1, near)):
                pltpu.make_async_remote_copy(
                    src_ref=piece(br, c), dst_ref=piece(bc, c), send_sem=c_send.at[slot, c],
                    recv_sem=c_recv.at[c], device_id=to, device_id_type=pl.DeviceIdType.MESH,
                ).start()

    def take(c):
        remote(piece(br, c), b_send.at[0, c], b_recv.at[c], right).wait_recv()
        pass_on(piece(br, c), b_send, b_recv, c)
        give(c)

    def forward(c):
        @pl.when(relay)
        def _():
            remote(piece(bc, c), c_send.at[0, c], c_recv.at[c], far).wait_recv()
            remote(piece(bc, c), c_send.at[1, c], c_recv.at[c], near).start()

    give(column)
    between = {}
    between[1] = [functools.partial(at_distance, 1, take)]
    between[2] = [functools.partial(forward, column)]
    between[3] = [functools.partial(at_distance, 2, take)]
    between[4] = [functools.partial(at_distance, 1, forward)]
    between[5] = [functools.partial(at_distance, d, take) for d in range(3, columns)]
    between[6] = [functools.partial(at_distance, d, forward) for d in range(2, columns)]
    factor_in_place(a, w, between)
    for c in range(columns):

        @pl.when(from_near)
        def _(c=c):
            remote(piece(bc, c), c_send.at[0, c], c_recv.at[c], near).wait_recv()

        @pl.when(relay)
        def _(c=c):
            remote(piece(bc, c), c_send.at[1, c], c_recv.at[c], near).wait_send()

        @pl.when(root)
        def _(c=c):
            remote(piece(br, c), c_send.at[0, c], c_recv.at[c], far).wait_send()
            remote(piece(br, c), c_send.at[1, c], c_recv.at[c], near).wait_send()

        passed(piece(br, c), b_send, b_recv, c)

    @pl.when(root)
    def _():
        bc[...] = br[...]


    factor_ref[...] = a[pl.ds(pl.multiple_of((row * columns + column) * share, share), share), :]
    solve_sides(a, w, br, bc, xh, xl, lh, ll)
    own_t.wait()

    def owner(g, r, b):
        return (map_ref[g, r * blocks + b] % quarter) // per_owner

    mine = [owner(child, row, b) for b in range(blocks)]

    def pick(to, slot):
        block, rank = jnp.int32(0), jnp.int32(0)
        for b in range(blocks):
            here = mine[b] == to
            block = jnp.where(here & (rank == slot), b, block)
            rank += here.astype(jnp.int32)
        return block

    def give_away(s, d):
        return pltpu.make_async_remote_copy(
            src_ref=stage.at[s], dst_ref=piece_ref.at[blocks + s],
            send_sem=x_send.at[s], recv_sem=x_recv.at[s],
            device_id={"wide": lax.rem(child + d, owners)}, device_id_type=pl.DeviceIdType.MESH,
        )

    slots = [(d, i) for d in range(1, owners) for i in range(sure)]
    columns_side = tuple(x[blocks:].reshape(q, x.shape[2]) for x in (xh, xl))
    for first in range(0, len(slots), 2):
        group = slots[first : first + 2]
        at = [pick(lax.rem(child + d, owners), i) for d, i in group]
        sides = tuple(jnp.concatenate([x[p] for p in at], axis=0) for x in (xh, xl))
        product = split_dot(sides, columns_side, NT)
        for n, (p, (d, _)) in enumerate(zip(at, group)):
            stage[first + n] = t[p] - product[n * BLOCK : n * BLOCK + BLOCK, :]
            give_away(first + n, d).start()
    panel_ref[...] = br[pl.ds(pl.multiple_of(column * part, part), part), :]
    step = 3 if blocks % 3 == 0 else 1
    for first in range(0, blocks, step):
        low, high = first * BLOCK, (first + step) * BLOCK
        rows_side = tuple(x[first : first + step].reshape(high - low, x.shape[2]) for x in (xh, xl))
        product = split_dot(rows_side, columns_side, NT)
        for b in range(first, first + step):
            o = b * BLOCK
            piece_ref[b] = t[b] - product[o - low : o - low + BLOCK, :]
    need = jnp.int32(0)
    if sure < most_slots(blocks, per_owner):
        for g in range(owners):
            for r in range(rows):
                there = [owner(g, r, b) for b in range(blocks)]
                for e in range(owners):
                    if e != g:
                        need = jnp.maximum(need, sum((x == e).astype(jnp.int32) for x in there))
    need_ref[0] = need
    for s, (d, _) in enumerate(slots):
        give_away(s, d).wait()


def front_call(row_map, diag, lower, trailing, rows, columns, owners, sure, quarter):
    n = diag.shape[1]
    share, part = diag.shape[0], lower.shape[0]
    q = part * columns
    blocks = q // BLOCK
    dma = pltpu.SemaphoreType.DMA
    away = (owners - 1) * sure
    return pl.pallas_call(
        functools.partial(front_kernel, rows, columns, owners, sure, quarter),
        name="front",
        out_shape=(
            jax.ShapeDtypeStruct((share, n), F32),
            jax.ShapeDtypeStruct((part, n), F32),
            jax.ShapeDtypeStruct((blocks + away, BLOCK, q), F32),
            jax.ShapeDtypeStruct((1,), jnp.int32),
        ),
        in_specs=[SMEM] + [pl.BlockSpec(memory_space=pl.ANY)] * 3,
        out_specs=(VMEM,) * 3 + (SMEM,),
        scratch_shapes=[
            pltpu.VMEM((n, n), F32),
            pltpu.VMEM((n // BLOCK, BLOCK, BLOCK), F32),
            pltpu.VMEM((q, n), F32),
            pltpu.VMEM((q, n), F32),
            pltpu.VMEM((2 * blocks, BLOCK, n), BF16),
            pltpu.VMEM((2 * blocks, BLOCK, n), BF16),
            pltpu.VMEM((n, n), BF16),
            pltpu.VMEM((n, n), BF16),
            pltpu.VMEM((blocks, BLOCK, q), F32),
            pltpu.VMEM((away, BLOCK, q), F32),
            dma((away,)), dma((away,)),
            dma((3,)), dma((2, columns)), dma((columns,)), dma((columns,)), dma((columns,)),
            dma((2, columns)), dma((2, columns)), dma((2, columns)), dma((columns,)),
            dma((2, columns)), dma((columns,)),
        ],
        compiler_params=pltpu.CompilerParams(
            vmem_limit_bytes=56 << 20, collective_id=0, has_side_effects=True
        ),
    )(row_map, diag, lower, trailing.reshape(blocks, BLOCK, q))


def rest_kernel(owners, sure, more, quarter, map_ref, piece_ref, out_ref, stage, send, recv):
    child, row = lax.axis_index("wide"), lax.axis_index("grow")
    blocks = out_ref.shape[2] // BLOCK
    per_owner = quarter // owners
    barrier = pltpu.get_barrier_semaphore()
    for d in range(1, owners):
        pl.semaphore_signal(
            barrier, inc=1, device_id={"wide": lax.rem(child + d, owners)},
            device_id_type=pl.DeviceIdType.MESH,
        )
    mine = [(map_ref[child, row * blocks + b] % quarter) // per_owner for b in range(blocks)]

    def give_away(s, d):
        return pltpu.make_async_remote_copy(
            src_ref=stage.at[s], dst_ref=out_ref.at[s], send_sem=send.at[s], recv_sem=recv.at[s],
            device_id={"wide": lax.rem(child + d, owners)}, device_id_type=pl.DeviceIdType.MESH,
        )

    slots = [(d, sure + i) for d in range(1, owners) for i in range(more)]
    for s, (d, slot) in enumerate(slots):
        block, rank = jnp.int32(0), jnp.int32(0)
        for b in range(blocks):
            here = mine[b] == lax.rem(child + d, owners)
            block = jnp.where(here & (rank == slot), b, block)
            rank += here.astype(jnp.int32)
        stage[s] = piece_ref[block]
    pl.semaphore_wait(barrier, owners - 1)
    for s, (d, _) in enumerate(slots):
        give_away(s, d).start()
    for s, (d, _) in enumerate(slots):
        give_away(s, d).wait()


def rest_call(row_map, pieces, owners, sure, more, quarter):
    away = (owners - 1) * more
    shape = (away,) + pieces.shape[1:]
    dma = pltpu.SemaphoreType.DMA
    return pl.pallas_call(
        functools.partial(rest_kernel, owners, sure, more, quarter),
        name="rest",
        out_shape=jax.ShapeDtypeStruct(shape, F32),
        in_specs=[SMEM, VMEM],
        out_specs=VMEM,
        scratch_shapes=[pltpu.VMEM(shape, F32), dma((away,)), dma((away,))],
        compiler_params=pltpu.CompilerParams(
            vmem_limit_bytes=12 << 20, collective_id=1, has_side_effects=True
        ),
    )(row_map, pieces)


def add_kernel(owners, sure, map_ref, parent_ref, *refs):
    pieces, out_ref = refs[:-1], refs[-1]
    p = pl.program_id(0)
    per_owner = pl.num_programs(0)
    quarter = owners * per_owner
    q = pieces[0].shape[2]
    blocks = q // BLOCK
    column_blocks = out_ref.shape[2] // BLOCK
    child, row = lax.axis_index("wide"), lax.axis_index("grow")
    column = lax.axis_index("gcol")
    out_ref[...] = parent_ref[...]

    def add(g, carry):
        block, slot, rank = jnp.int32(-1), jnp.int32(-1), jnp.int32(0)
        for b in range(blocks):
            to = map_ref[g, row * blocks + b] % quarter
            hit = to == child * per_owner + p
            block = jnp.where(hit, b, block)
            slot = jnp.where(hit, rank, slot)
            rank += (to // per_owner == child).astype(jnp.int32)
        away = lax.rem(child - g + owners, owners) - 1

        def put(ref, index):
            for b in range(blocks):
                to = map_ref[g, column * blocks + b] % column_blocks
                at = pl.ds(pl.multiple_of(to * BLOCK, BLOCK), BLOCK)
                out_ref[0, :, at] += ref[index, :, b * BLOCK : b * BLOCK + BLOCK]

        more = most_slots(blocks, per_owner) - sure

        @pl.when((block >= 0) & ((g == child) | (slot < sure)))
        def _():
            put(pieces[0], jnp.where(g == child, block, blocks + away * sure + slot))

        if len(pieces) > 1:

            @pl.when((block >= 0) & (g != child) & (slot >= sure))
            def _():
                put(pieces[1], away * more + slot - sure)

        return carry

    lax.fori_loop(0, owners, add, 0)


def add_call(row_map, parent, pieces, owners, sure):
    _, rows, width = parent.shape
    block = pl.BlockSpec((1, BLOCK, width), lambda p: (0, p, 0))
    return pl.pallas_call(
        functools.partial(add_kernel, owners, sure),
        name="extend_add",
        out_shape=jax.ShapeDtypeStruct(parent.shape, F32),
        grid=(rows // BLOCK,),
        in_specs=[SMEM, block] + [VMEM] * len(pieces),
        out_specs=block,
        compiler_params=pltpu.CompilerParams(vmem_limit_bytes=20 << 20),
    )(row_map, parent, *pieces)


def body(diag_block, lower_block, trailing_block, parent_front, row_map):
    owners = lax.axis_size("wide")
    rows, columns = lax.axis_size("grow"), lax.axis_size("gcol")
    quarter = parent_front.shape[1] * owners // BLOCK
    blocks = trailing_block.shape[1] // BLOCK
    most = most_slots(blocks, quarter // owners)
    sure = max(1, 2 * most // 3)
    factor, panel, pieces, need = front_call(
        row_map, diag_block[0], lower_block[0], trailing_block[0], rows, columns, owners, sure, quarter,
    )

    def few():
        return add_call(row_map, parent_front, (pieces,), owners, sure)

    def many():
        rest = rest_call(row_map, pieces, owners, sure, most - sure, quarter)
        return add_call(row_map, parent_front, (pieces, rest), owners, sure)

    parent = lax.cond(need[0] > sure, many, few) if most > sure else few()
    return (factor[None], panel[None], parent)


def solution(mesh):
    placed = (
        P("wide", ("grow", "gcol"), None),
        P("wide", ("grow", "gcol"), None),
        P("wide", "grow", "gcol"),
        P("grow", "wide", "gcol"),
        P(),
    )
    return jax.shard_map(
        body,
        mesh=mesh,
        in_specs=placed,
        out_specs=(
            P("wide", ("grow", "gcol"), None),
            P("wide", ("grow", "gcol"), None),
            P("grow", "wide", "gcol"),
        ),
        check_vma=False,
    )
```

```python
import functools
import math

import jax
import jax.numpy as jnp
from jax import lax
from jax.experimental import pallas as pl
from jax.experimental.pallas import tpu as pltpu
from jax.sharding import PartitionSpec as P

BLOCK = 128
HALF = 64
F32 = jnp.float32
BF16 = jnp.bfloat16
NT = (((1,), (1,)), ((), ()))
NN = (((1,), (0,)), ((), ()))
VMEM = pl.BlockSpec(memory_space=pltpu.VMEM)
SMEM = pl.BlockSpec(memory_space=pltpu.SMEM)


def full_dot(a, b, dims):
    return lax.dot_general(
        a, b, dims, precision=lax.Precision.HIGHEST, preferred_element_type=F32
    )


def parts(x):
    high = x.astype(BF16)
    return high, (x - high.astype(F32)).astype(BF16)


def split_dot(a, b, dims):
    one = functools.partial(lax.dot_general, dimension_numbers=dims, preferred_element_type=F32)
    return one(a[0], b[0]) + (one(a[0], b[1]) + one(a[1], b[0]))


def factor_half(block):
    half = block.shape[0]
    rows = lax.broadcasted_iota(jnp.int32, (half, half), 0)
    cols = lax.broadcasted_iota(jnp.int32, (half, half), 1)
    eye = jnp.where(rows == cols, 1.0, 0.0).astype(F32)
    full = jnp.concatenate([block, eye], axis=1)
    count = half // 8
    wide = (8, 2 * half)
    groups = [full[8 * s : 8 * s + 8] for s in range(count)]
    sub = lax.broadcasted_iota(jnp.int32, wide, 0)
    at_row = [jnp.full(wide, i, jnp.int32) for i in range(8)]
    spread = lambda x: jnp.broadcast_to(x, wide)
    take = lambda x, i: jnp.take_along_axis(x, at_row[i], axis=0, mode="promise_in_bounds")
    done = []
    for s in range(count):
        c = 8 * s
        column = {
            t: [spread(groups[t][:, c + j : c + j + 1]) for j in range(8)] for t in range(s, count)
        }
        lead = [spread(groups[s][i : i + 1, :]) for i in range(8)]
        pivot = {(i, j): take(column[s][j], i) for i in range(8) for j in range(i, 8)}
        below = range(s + 1, count)
        keep = jnp.zeros(wide, F32)
        for j in range(8):
            r = lax.rsqrt(pivot[j, j])
            unit = lead[j] * r
            mult = {i: pivot[j, i] * r for i in range(j + 1, 8)}
            for i in range(j + 1, 8):
                for q in range(i, 8):
                    pivot[i, q] = pivot[i, q] - mult[i] * mult[q]
                lead[i] = lead[i] - mult[i] * unit
            for t in below:
                m = column[t][j] * r
                for i in range(j + 1, 8):
                    column[t][i] = column[t][i] - m * mult[i]
                groups[t] = groups[t] - m * unit
            keep = jnp.where(sub == j, unit, keep)
        done.append(keep)
    both = jnp.concatenate(done, axis=0)
    upper = jnp.where(rows <= cols, both[:, :half], 0.0)
    inverse = jnp.where(rows >= cols, both[:, half:], 0.0)
    return upper.T, inverse


def square(a, b, c):
    return jnp.concatenate(
        [
            jnp.concatenate([a, jnp.zeros_like(a)], axis=1),
            jnp.concatenate([b, c], axis=1),
        ],
        axis=0,
    )


def factor_in_place(a, w, between):
    n = a.shape[0]
    count = n // BLOCK

    def step(k, carry):
        o = pl.multiple_of(k * BLOCK, BLOCK)
        d = a[pl.ds(o, BLOCK), pl.ds(o, BLOCK)]
        l1, w1 = factor_half(d[:HALF, :HALF])
        l21 = full_dot(d[HALF:, :HALF], w1, NT)
        l2, w2 = factor_half(d[HALF:, HALF:] - full_dot(l21, l21, NT))
        w21 = -full_dot(w2, full_dot(l21, w1, NN), NN)
        a[pl.ds(o, BLOCK), pl.ds(o, BLOCK)] = square(l1, l21, l2)
        w[k] = square(w1, w21, w2)
        for at in range(count - 1):

            @pl.when(k == at)
            def _(at=at):
                low, high = at * BLOCK, at * BLOCK + BLOCK
                a[low:high, high:] = jnp.zeros((BLOCK, n - high), F32)
                p = split_dot(parts(a[high:, low:high]), parts(w[at]), NT)
                a[high:, low:high] = p
                ph, pl_ = parts(p)
                for c in range(high, n, 2 * BLOCK):
                    e = min(c + 2 * BLOCK, n)
                    left, right = slice(c - high, None), slice(c - high, e - high)
                    a[c:, c:e] = a[c:, c:e] - split_dot(
                        (ph[left], pl_[left]), (ph[right], pl_[right]), NT
                    )
                for act in between.get(at, ()):
                    act()

        return carry

    lax.fori_loop(0, count, step, 0)


def most_slots(blocks, per_owner):
    return min(blocks, per_owner)


def invert_pairs(l_ref, w_ref, lh, ll, wh, wl):
    pair = 2 * BLOCK
    lh[...], ll[...] = parts(l_ref[...])
    for k in range(l_ref.shape[0] // pair):
        low, high = k * pair, k * pair + pair
        wa, wb = w_ref[2 * k], w_ref[2 * k + 1]
        across = l_ref[low + BLOCK : high, low : low + BLOCK]
        wh[k], wl[k] = parts(square(wa, -full_dot(wb, full_dot(across, wa, NN), NN), wb))


def solve_rows(b_ref, xh, xl, lh, ll, wh, wl, keep):
    n = lh.shape[0]
    blocks = xh.shape[0]
    grain = b_ref.shape[1]
    few = next(f for f in (2, 3, 1) if blocks % f == 0)
    tile, pair = few * BLOCK, 2 * BLOCK
    for k in range(n // pair):
        low, high = k * pair, k * pair + pair

        def solve(i, carry, k=k, low=low, high=high):
            at = pl.ds(i * few, few)
            from_at = pl.ds(i * (tile // grain), tile // grain)
            rest = b_ref[from_at, :, low:high].reshape(tile, pair)
            if low:
                left = tuple(x[at, :, :low].reshape(tile, low) for x in (xh, xl))
                rest = rest - split_dot(left, (lh[low:high, :low], ll[low:high, :low]), NT)
            x = split_dot(parts(rest), (wh[k], wl[k]), NT)
            for ref, value in zip((xh, xl), parts(x)):
                ref[at, :, low:high] = value.reshape(few, BLOCK, pair)
            if keep:
                b_ref[from_at, :, low:high] = x.reshape(tile // grain, grain, pair)
            return carry

        lax.fori_loop(0, blocks // few, solve, 0)


def front_kernel(
    rows, columns, owners, sure, quarter, map_ref, d_ref, x_ref, t_ref,
    factor_ref, panel_ref, piece_ref, need_ref,
    a, w, br, side, xh, xl, yh, yl, lh, ll, wh, wl, t, stage, x_send, x_recv,
    local, line_send, line_recv, far_send, far_recv, near_send, near_recv,
    b_send, b_recv, c_send, c_recv,
):
    child = lax.axis_index("wide")
    row, column = lax.axis_index("grow"), lax.axis_index("gcol")
    q = br.shape[0] * br.shape[1]
    blocks = q // BLOCK
    grain = br.shape[1]
    bc = side.at[pl.ds(0, q // grain)]
    half = a.shape[1] // 2
    per_owner = quarter // owners
    far_row = lax.rem(row + rows // 2, rows)
    near_row = row + 1 - 2 * lax.rem(row, 2)
    right, left = {"gcol": column + 1}, {"gcol": column - 1}
    far, near = {"grow": far_row}, {"grow": near_row}
    share, part = d_ref.shape[0], x_ref.shape[0] * x_ref.shape[1]
    has_left, has_right = column > 0, column < columns - 1

    def band(r, c):
        return a.at[pl.ds(pl.multiple_of((r * columns + c) * share, share), share)]

    def cross(r, c):
        side_of = pl.multiple_of((r // (rows // 2)) * half, half)
        rows_of = pl.ds(pl.multiple_of((r * columns + c) * share, share), share)
        return a.at[rows_of, pl.ds(side_of, half)]

    def piece(ref, c):
        return ref.at[pl.ds(c * (part // grain), part // grain)]

    def remote(ref, send, recv, to):
        return pltpu.make_async_remote_copy(
            src_ref=ref, dst_ref=ref, send_sem=send, recv_sem=recv,
            device_id=to, device_id_type=pl.DeviceIdType.MESH,
        )

    own_d = pltpu.make_async_copy(d_ref, band(row, column), local.at[0])
    own_x = pltpu.make_async_copy(x_ref, piece(br, column), local.at[1])
    own_t = pltpu.make_async_copy(t_ref, t, local.at[2])
    own_d.start()
    own_x.start()
    own_t.start()
    barrier = pltpu.get_barrier_semaphore()
    next_column = {"gcol": lax.rem(column + 1, columns)}
    last_column = {"gcol": lax.rem(column + columns - 1, columns)}
    for to in (far, near, next_column, last_column):
        pl.semaphore_signal(barrier, inc=1, device_id=to, device_id_type=pl.DeviceIdType.MESH)
    for d in range(1, owners):
        pl.semaphore_signal(
            barrier, inc=1, device_id={"wide": lax.rem(child + d, owners)},
            device_id_type=pl.DeviceIdType.MESH,
        )
    pl.semaphore_wait(barrier, 3 + owners)
    own_d.wait()
    own_x.wait()

    def pass_on(ref, send, recv, c, both=False):
        @pl.when((c <= column) & has_right)
        def _():
            remote(ref, send.at[0, c], recv.at[c], right).start()

        @pl.when((c >= column) & has_left)
        def _():
            remote(ref, send.at[1, c], recv.at[c], left).start()

    def passed(ref, send, recv, c):
        @pl.when((c <= column) & has_right)
        def _():
            remote(ref, send.at[0, c], recv.at[c], right).wait_send()

        @pl.when((c >= column) & has_left)
        def _():
            remote(ref, send.at[1, c], recv.at[c], left).wait_send()

    def at_distance(d, act):
        for c, there in ((column - d, column - d >= 0), (column + d, column + d < columns)):
            pl.when(there)(functools.partial(act, c))

    def spread(c):
        remote(cross(row, c), far_send.at[c], far_recv.at[c], far).start()
        remote(band(row, c), near_send.at[0, c], near_recv.at[0, c], near).start()

    pass_on(band(row, column), line_send, line_recv, column)
    spread(column)

    def arrived(c):
        remote(band(row, c), line_send.at[0, c], line_recv.at[c], right).wait_recv()
        pass_on(band(row, c), line_send, line_recv, c)
        spread(c)

    def crossed(c):
        remote(cross(far_row, c), far_send.at[c], far_recv.at[c], far).wait_recv()
        remote(cross(far_row, c), near_send.at[1, c], near_recv.at[1, c], near).start()

    at_distance(1, arrived)
    crossed(column)
    for d in range(2, columns):
        at_distance(d, arrived)
        at_distance(d - 1, crossed)
    pass_on(piece(br, column), b_send, b_recv, column)
    at_distance(columns - 1, crossed)
    near_far_row = lax.rem(near_row + rows // 2, rows)
    for c in range(columns):
        remote(band(near_row, c), near_send.at[0, c], near_recv.at[0, c], near).wait_recv()
        remote(cross(near_far_row, c), near_send.at[1, c], near_recv.at[1, c], near).wait_recv()
    for c in range(columns):
        remote(cross(row, c), far_send.at[c], far_recv.at[c], far).wait_send()
        remote(band(row, c), near_send.at[0, c], near_recv.at[0, c], near).wait_send()
        remote(cross(far_row, c), near_send.at[1, c], near_recv.at[1, c], near).wait_send()
        passed(band(row, c), line_send, line_recv, c)

    root = row == column
    relay = far_row == column
    from_far = relay
    from_near = jnp.logical_not(root | relay)

    def give(c):
        @pl.when(root)
        def _():
            for slot, to in ((0, far), (1, near)):
                pltpu.make_async_remote_copy(
                    src_ref=piece(br, c), dst_ref=piece(bc, c), send_sem=c_send.at[slot, c],
                    recv_sem=c_recv.at[c], device_id=to, device_id_type=pl.DeviceIdType.MESH,
                ).start()

    def take(c):
        remote(piece(br, c), b_send.at[0, c], b_recv.at[c], right).wait_recv()
        pass_on(piece(br, c), b_send, b_recv, c)
        give(c)

    def forward(c):
        @pl.when(relay)
        def _():
            remote(piece(bc, c), c_send.at[0, c], c_recv.at[c], far).wait_recv()
            remote(piece(bc, c), c_send.at[1, c], c_recv.at[c], near).start()

    give(column)

    @pl.when(row < rows // 2)
    def _():
        for i in range(0, half, BLOCK):
            for j in range(0, half, BLOCK):
                a[half + i : half + i + BLOCK, j : j + BLOCK] = (
                    a[j : j + BLOCK, half + i : half + i + BLOCK].T
                )

    between = {}
    between[1] = [functools.partial(at_distance, 1, take)]
    between[2] = [functools.partial(forward, column)]
    between[4] = [functools.partial(at_distance, 2, take)]
    between[5] = [functools.partial(at_distance, 1, forward)]
    factor_in_place(a, w, between)
    for d in range(3, columns):
        at_distance(d, take)
    for d in range(2, columns):
        at_distance(d, forward)
    factor_ref[...] = a[pl.ds(pl.multiple_of((row * columns + column) * share, share), share), :]
    invert_pairs(a, w, lh, ll, wh, wl)
    for c in range(columns):

        @pl.when(from_near)
        def _(c=c):
            remote(piece(bc, c), c_send.at[0, c], c_recv.at[c], near).wait_recv()

        @pl.when(relay)
        def _(c=c):
            remote(piece(bc, c), c_send.at[1, c], c_recv.at[c], near).wait_send()

        @pl.when(root)
        def _(c=c):
            remote(piece(br, c), c_send.at[0, c], c_recv.at[c], far).wait_send()
            remote(piece(br, c), c_send.at[1, c], c_recv.at[c], near).wait_send()

        passed(piece(br, c), b_send, b_recv, c)

    @pl.when(root)
    def _():
        bc[...] = br[...]

    own_t.wait()

    def owner(g, r, b):
        return (map_ref[g, r * blocks + b] % quarter) // per_owner

    mine = [owner(child, row, b) for b in range(blocks)]

    def pick(to, slot):
        block, rank = jnp.int32(0), jnp.int32(0)
        for b in range(blocks):
            here = mine[b] == to
            block = jnp.where(here & (rank == slot), b, block)
            rank += here.astype(jnp.int32)
        return block

    def give_away(s, d):
        return pltpu.make_async_remote_copy(
            src_ref=stage.at[s], dst_ref=piece_ref.at[blocks + s],
            send_sem=x_send.at[s], recv_sem=x_recv.at[s],
            device_id={"wide": lax.rem(child + d, owners)}, device_id_type=pl.DeviceIdType.MESH,
        )

    slots = [(d, i) for d in range(1, owners) for i in range(sure)]
    picked = [pick(lax.rem(child + d, owners), i) for d, i in slots]
    each = BLOCK // grain
    ahead = xh.shape[0] > blocks
    for s, block in enumerate(picked if ahead else ()):
        for h in range(each):
            side[q // grain + s * each + h] = br[block * each + h]
    if not ahead:
        solve_rows(br, yh, yl, lh, ll, wh, wl, True)
    solve_rows(side, xh, xl, lh, ll, wh, wl, False)
    columns_side = tuple(x[:blocks].reshape(q, x.shape[2]) for x in (xh, xl))
    for first in range(0, len(slots), 2):
        last = min(first + 2, len(slots))
        count = last - first
        if ahead:
            sides = tuple(
                x[blocks + first : blocks + last].reshape(count * BLOCK, x.shape[2])
                for x in (xh, xl)
            )
        else:
            sides = tuple(
                jnp.concatenate([y[block] for block in picked[first:last]], axis=0)
                for y in (yh, yl)
            )
        product = split_dot(sides, columns_side, NT)
        for n in range(count):
            stage[first + n] = t[picked[first + n]] - product[n * BLOCK : n * BLOCK + BLOCK, :]
            give_away(first + n, slots[first + n][0]).start()
    if ahead:
        solve_rows(br, yh, yl, lh, ll, wh, wl, True)
    panel_ref[...] = br[pl.ds(column * (part // grain), part // grain)].reshape(part, a.shape[1])
    step = 3 if blocks % 3 == 0 else 1
    for first in range(0, blocks, step):
        low, high = first * BLOCK, (first + step) * BLOCK
        rows_side = tuple(x[first : first + step].reshape(high - low, x.shape[2]) for x in (yh, yl))
        product = split_dot(rows_side, columns_side, NT)
        for b in range(first, first + step):
            o = b * BLOCK
            piece_ref[b] = t[b] - product[o - low : o - low + BLOCK, :]
    need = jnp.int32(0)
    if sure < most_slots(blocks, per_owner):
        for g in range(owners):
            for r in range(rows):
                there = [owner(g, r, b) for b in range(blocks)]
                for e in range(owners):
                    if e != g:
                        need = jnp.maximum(need, sum((x == e).astype(jnp.int32) for x in there))
    need_ref[0] = need
    for s, (d, _) in enumerate(slots):
        give_away(s, d).wait()


def front_call(row_map, diag, lower, trailing, rows, columns, owners, sure, quarter):
    n = diag.shape[1]
    share, part = diag.shape[0], lower.shape[0]
    q = part * columns
    blocks = q // BLOCK
    dma = pltpu.SemaphoreType.DMA
    away = (owners - 1) * sure
    grain = math.gcd(part, BLOCK)
    ahead = away if away < blocks else 0
    return pl.pallas_call(
        functools.partial(front_kernel, rows, columns, owners, sure, quarter),
        name="front",
        out_shape=(
            jax.ShapeDtypeStruct((share, n), F32),
            jax.ShapeDtypeStruct((part, n), F32),
            jax.ShapeDtypeStruct((blocks + away, BLOCK, q), F32),
            jax.ShapeDtypeStruct((1,), jnp.int32),
        ),
        in_specs=[SMEM] + [pl.BlockSpec(memory_space=pl.ANY)] * 3,
        out_specs=(VMEM,) * 3 + (SMEM,),
        scratch_shapes=[
            pltpu.VMEM((n, n), F32),
            pltpu.VMEM((n // BLOCK, BLOCK, BLOCK), F32),
            pltpu.VMEM((q // grain, grain, n), F32),
            pltpu.VMEM(((q + ahead * BLOCK) // grain, grain, n), F32),
            pltpu.VMEM((blocks + ahead, BLOCK, n), BF16),
            pltpu.VMEM((blocks + ahead, BLOCK, n), BF16),
            pltpu.VMEM((blocks, BLOCK, n), BF16),
            pltpu.VMEM((blocks, BLOCK, n), BF16),
            pltpu.VMEM((n, n), BF16),
            pltpu.VMEM((n, n), BF16),
            pltpu.VMEM((n // (2 * BLOCK), 2 * BLOCK, 2 * BLOCK), BF16),
            pltpu.VMEM((n // (2 * BLOCK), 2 * BLOCK, 2 * BLOCK), BF16),
            pltpu.VMEM((blocks, BLOCK, q), F32),
            pltpu.VMEM((away, BLOCK, q), F32),
            dma((away,)), dma((away,)),
            dma((3,)), dma((2, columns)), dma((columns,)), dma((columns,)), dma((columns,)),
            dma((2, columns)), dma((2, columns)), dma((2, columns)), dma((columns,)),
            dma((2, columns)), dma((columns,)),
        ],
        compiler_params=pltpu.CompilerParams(
            vmem_limit_bytes=56 << 20, collective_id=0, has_side_effects=True
        ),
    )(
        row_map, diag, lower.reshape(part // grain, grain, n), trailing.reshape(blocks, BLOCK, q)
    )


def rest_kernel(owners, sure, more, quarter, map_ref, piece_ref, out_ref, stage, send, recv):
    child, row = lax.axis_index("wide"), lax.axis_index("grow")
    blocks = out_ref.shape[2] // BLOCK
    per_owner = quarter // owners
    barrier = pltpu.get_barrier_semaphore()
    for d in range(1, owners):
        pl.semaphore_signal(
            barrier, inc=1, device_id={"wide": lax.rem(child + d, owners)},
            device_id_type=pl.DeviceIdType.MESH,
        )
    mine = [(map_ref[child, row * blocks + b] % quarter) // per_owner for b in range(blocks)]

    def give_away(s, d):
        return pltpu.make_async_remote_copy(
            src_ref=stage.at[s], dst_ref=out_ref.at[s], send_sem=send.at[s], recv_sem=recv.at[s],
            device_id={"wide": lax.rem(child + d, owners)}, device_id_type=pl.DeviceIdType.MESH,
        )

    slots = [(d, sure + i) for d in range(1, owners) for i in range(more)]
    for s, (d, slot) in enumerate(slots):
        block, rank = jnp.int32(0), jnp.int32(0)
        for b in range(blocks):
            here = mine[b] == lax.rem(child + d, owners)
            block = jnp.where(here & (rank == slot), b, block)
            rank += here.astype(jnp.int32)
        stage[s] = piece_ref[block]
    pl.semaphore_wait(barrier, owners - 1)
    for s, (d, _) in enumerate(slots):
        give_away(s, d).start()
    for s, (d, _) in enumerate(slots):
        give_away(s, d).wait()


def rest_call(row_map, pieces, owners, sure, more, quarter):
    away = (owners - 1) * more
    shape = (away,) + pieces.shape[1:]
    dma = pltpu.SemaphoreType.DMA
    return pl.pallas_call(
        functools.partial(rest_kernel, owners, sure, more, quarter),
        name="rest",
        out_shape=jax.ShapeDtypeStruct(shape, F32),
        in_specs=[SMEM, VMEM],
        out_specs=VMEM,
        scratch_shapes=[pltpu.VMEM(shape, F32), dma((away,)), dma((away,))],
        compiler_params=pltpu.CompilerParams(
            vmem_limit_bytes=12 << 20, collective_id=more, has_side_effects=True
        ),
    )(row_map, pieces)


def add_kernel(owners, sure, more, map_ref, parent_ref, *refs):
    pieces, out_ref = refs[:-1], refs[-1]
    p = pl.program_id(0)
    per_owner = pl.num_programs(0)
    quarter = owners * per_owner
    q = pieces[0].shape[2]
    blocks = q // BLOCK
    column_blocks = out_ref.shape[2] // BLOCK
    child, row = lax.axis_index("wide"), lax.axis_index("grow")
    column = lax.axis_index("gcol")
    out_ref[...] = parent_ref[...]

    def add(g, carry):
        block, slot, rank = jnp.int32(-1), jnp.int32(-1), jnp.int32(0)
        for b in range(blocks):
            to = map_ref[g, row * blocks + b] % quarter
            hit = to == child * per_owner + p
            block = jnp.where(hit, b, block)
            slot = jnp.where(hit, rank, slot)
            rank += (to // per_owner == child).astype(jnp.int32)
        away = lax.rem(child - g + owners, owners) - 1

        def put(ref, index):
            for b in range(blocks):
                to = map_ref[g, column * blocks + b] % column_blocks
                at = pl.ds(pl.multiple_of(to * BLOCK, BLOCK), BLOCK)
                out_ref[0, :, at] += ref[index, :, b * BLOCK : b * BLOCK + BLOCK]

        @pl.when((block >= 0) & ((g == child) | (slot < sure)))
        def _():
            put(pieces[0], jnp.where(g == child, block, blocks + away * sure + slot))

        if len(pieces) > 1:

            @pl.when((block >= 0) & (g != child) & (slot >= sure))
            def _():
                put(pieces[1], away * more + slot - sure)

        return carry

    lax.fori_loop(0, owners, add, 0)


def add_call(row_map, parent, pieces, owners, sure, more):
    _, rows, width = parent.shape
    block = pl.BlockSpec((1, BLOCK, width), lambda p: (0, p, 0))
    return pl.pallas_call(
        functools.partial(add_kernel, owners, sure, more),
        name="extend_add",
        out_shape=jax.ShapeDtypeStruct(parent.shape, F32),
        grid=(rows // BLOCK,),
        in_specs=[SMEM, block] + [VMEM] * len(pieces),
        out_specs=block,
        compiler_params=pltpu.CompilerParams(vmem_limit_bytes=20 << 20),
    )(row_map, parent, *pieces)


def body(diag_block, lower_block, trailing_block, parent_front, row_map):
    owners = lax.axis_size("wide")
    rows, columns = lax.axis_size("grow"), lax.axis_size("gcol")
    quarter = parent_front.shape[1] * owners // BLOCK
    blocks = trailing_block.shape[1] // BLOCK
    most = most_slots(blocks, quarter // owners)
    sure = max(1, 2 * most // 3)
    factor, panel, pieces, need = front_call(
        row_map, diag_block[0], lower_block[0], trailing_block[0], rows, columns, owners, sure, quarter,
    )

    def finish(more):
        def run():
            extra = (rest_call(row_map, pieces, owners, sure, more, quarter),) if more else ()
            return add_call(row_map, parent_front, (pieces,) + extra, owners, sure, more)

        return run

    branches = [finish(more) for more in range(most - sure + 1)]
    parent = lax.switch(jnp.clip(need[0] - sure, 0, most - sure), branches)
    return (factor[None], panel[None], parent)


def solution(mesh):
    placed = (
        P("wide", ("grow", "gcol"), None),
        P("wide", ("grow", "gcol"), None),
        P("wide", "grow", "gcol"),
        P("grow", "wide", "gcol"),
        P(),
    )
    return jax.shard_map(
        body,
        mesh=mesh,
        in_specs=placed,
        out_specs=(
            P("wide", ("grow", "gcol"), None),
            P("wide", ("grow", "gcol"), None),
            P("grow", "wide", "gcol"),
        ),
        check_vma=False,
    )
```

```python
import functools
import math

import jax
import jax.numpy as jnp
from jax import lax
from jax.experimental import pallas as pl
from jax.experimental.pallas import tpu as pltpu
from jax.sharding import PartitionSpec as P

BLOCK = 128
HALF = 64
F32 = jnp.float32
BF16 = jnp.bfloat16
NT = (((1,), (1,)), ((), ()))
NN = (((1,), (0,)), ((), ()))
VMEM = pl.BlockSpec(memory_space=pltpu.VMEM)
SMEM = pl.BlockSpec(memory_space=pltpu.SMEM)


def full_dot(a, b, dims):
    return lax.dot_general(
        a, b, dims, precision=lax.Precision.HIGHEST, preferred_element_type=F32
    )


def parts(x):
    high = x.astype(BF16)
    return high, (x - high.astype(F32)).astype(BF16)


def split_dot(a, b, dims):
    one = functools.partial(lax.dot_general, dimension_numbers=dims, preferred_element_type=F32)
    return one(a[0], b[0]) + (one(a[0], b[1]) + one(a[1], b[0]))


def factor_half(block):
    half = block.shape[0]
    rows = lax.broadcasted_iota(jnp.int32, (half, half), 0)
    cols = lax.broadcasted_iota(jnp.int32, (half, half), 1)
    eye = jnp.where(rows == cols, 1.0, 0.0).astype(F32)
    full = jnp.concatenate([block, eye], axis=1)
    count = half // 8
    wide = (8, 2 * half)
    groups = [full[8 * s : 8 * s + 8] for s in range(count)]
    sub = lax.broadcasted_iota(jnp.int32, wide, 0)
    at_row = [jnp.full(wide, i, jnp.int32) for i in range(8)]
    spread = lambda x: jnp.broadcast_to(x, wide)
    take = lambda x, i: jnp.take_along_axis(x, at_row[i], axis=0, mode="promise_in_bounds")
    done = []
    for s in range(count):
        c = 8 * s
        column = {
            t: [spread(groups[t][:, c + j : c + j + 1]) for j in range(8)] for t in range(s, count)
        }
        lead = [spread(groups[s][i : i + 1, :]) for i in range(8)]
        pivot = {(i, j): take(column[s][j], i) for i in range(8) for j in range(i, 8)}
        below = range(s + 1, count)
        keep = jnp.zeros(wide, F32)
        for j in range(8):
            r = lax.rsqrt(pivot[j, j])
            unit = lead[j] * r
            mult = {i: pivot[j, i] * r for i in range(j + 1, 8)}
            for i in range(j + 1, 8):
                for q in range(i, 8):
                    pivot[i, q] = pivot[i, q] - mult[i] * mult[q]
                lead[i] = lead[i] - mult[i] * unit
            for t in below:
                m = column[t][j] * r
                for i in range(j + 1, 8):
                    column[t][i] = column[t][i] - m * mult[i]
                groups[t] = groups[t] - m * unit
            keep = jnp.where(sub == j, unit, keep)
        done.append(keep)
    both = jnp.concatenate(done, axis=0)
    upper = jnp.where(rows <= cols, both[:, :half], 0.0)
    inverse = jnp.where(rows >= cols, both[:, half:], 0.0)
    return upper.T, inverse


def square(a, b, c):
    return jnp.concatenate(
        [
            jnp.concatenate([a, jnp.zeros_like(a)], axis=1),
            jnp.concatenate([b, c], axis=1),
        ],
        axis=0,
    )


def factor_in_place(a, w, lh, ll, between):
    n = a.shape[0]
    count = n // BLOCK

    def step(k, carry):
        o = pl.multiple_of(k * BLOCK, BLOCK)
        d = a[pl.ds(o, BLOCK), pl.ds(o, BLOCK)]
        l1, w1 = factor_half(d[:HALF, :HALF])
        l21 = full_dot(d[HALF:, :HALF], w1, NT)
        l2, w2 = factor_half(d[HALF:, HALF:] - full_dot(l21, l21, NT))
        w21 = -full_dot(w2, full_dot(l21, w1, NN), NN)
        a[pl.ds(o, BLOCK), pl.ds(o, BLOCK)] = square(l1, l21, l2)
        w[k] = square(w1, w21, w2)
        for at in range(count - 1):

            @pl.when(k == at)
            def _(at=at):
                low, high = at * BLOCK, at * BLOCK + BLOCK
                a[low:high, high:] = jnp.zeros((BLOCK, n - high), F32)
                p = split_dot(parts(a[high:, low:high]), parts(w[at]), NT)
                a[high:, low:high] = p
                ph, pl_ = parts(p)
                lh[high:, low:high], ll[high:, low:high] = ph, pl_
                for c in range(high, n, 2 * BLOCK):
                    e = min(c + 2 * BLOCK, n)
                    left, right = slice(c - high, None), slice(c - high, e - high)
                    a[c:, c:e] = a[c:, c:e] - split_dot(
                        (ph[left], pl_[left]), (ph[right], pl_[right]), NT
                    )
                for act in between.get(at, ()):
                    act()

        return carry

    lax.fori_loop(0, count, step, 0)


def most_slots(blocks, per_owner):
    return min(blocks, per_owner)


def invert_diagonal(l_ref, w_ref, wh, wl):
    group = wh.shape[1]

    def inverse(at, size):
        if size == BLOCK:
            return w_ref[at // BLOCK]
        cut = size // 2
        first, second = inverse(at, cut), inverse(at + cut, cut)
        across = l_ref[at + cut : at + size, at : at + cut]
        product = parts(split_dot(parts(across), parts(first), NN))
        return square(first, -split_dot(parts(second), product, NN), second)

    for k in range(wh.shape[0]):
        wh[k], wl[k] = parts(inverse(k * group, group))


def front_kernel(
    rows, columns, owners, sure, quarter, map_ref, d_ref, x_ref, t_ref,
    factor_ref, panel_ref, piece_ref, need_ref,
    a, w, br, bc, xh, xl, yh, yl, lh, ll, wh, wl, t, stage, x_send, x_recv,
    local, line_send, line_recv, far_send, far_recv, near_send, near_recv,
    b_send, b_recv, c_send, c_recv,
):
    child = lax.axis_index("wide")
    row, column = lax.axis_index("grow"), lax.axis_index("gcol")
    n = a.shape[1]
    grain = br.shape[1]
    q = br.shape[0] * grain
    blocks = q // BLOCK
    per_owner = quarter // owners
    far_row = lax.rem(row + rows // 2, rows)
    near_row = row + 1 - 2 * lax.rem(row, 2)
    near_far_row = lax.rem(near_row + rows // 2, rows)
    right, left = {"gcol": column + 1}, {"gcol": column - 1}
    far, near = {"grow": far_row}, {"grow": near_row}
    share = d_ref.shape[0]
    grains = x_ref.shape[0]
    part = grains * grain
    has_left, has_right = column > 0, column < columns - 1

    def band(r, c):
        return pl.ds(pl.multiple_of((r * columns + c) * share, share), share)

    def cells(r, c, act):
        outer = (r == 0) | (r == rows - 1)
        start = jnp.where(outer, n // 2, jnp.where(r < rows // 2, 0, n // 4))
        act(0, a.at[band(r, c), pl.ds(pl.multiple_of(start, n // 4), n // 2)])
        extra = jnp.where(r == 0, 0, n // 4)
        slim = a.at[band(r, c), pl.ds(pl.multiple_of(extra, n // 4), n // 4)]
        pl.when(outer)(functools.partial(act, 1, slim))

    def remote(ref, send, recv, to):
        return pltpu.make_async_remote_copy(
            src_ref=ref, dst_ref=ref, send_sem=send, recv_sem=recv,
            device_id=to, device_id_type=pl.DeviceIdType.MESH,
        )

    own_d = pltpu.make_async_copy(d_ref, a.at[band(row, column)], local.at[0])
    own_x = pltpu.make_async_copy(x_ref, br.at[pl.ds(column * grains, grains)], local.at[1])
    own_t = pltpu.make_async_copy(t_ref, t, local.at[2])
    own_d.start()
    own_x.start()
    own_t.start()
    barrier = pltpu.get_barrier_semaphore()
    next_column = {"gcol": lax.rem(column + 1, columns)}
    last_column = {"gcol": lax.rem(column + columns - 1, columns)}
    others = [{"wide": lax.rem(child + d, owners)} for d in range(1, owners)]
    for to in [far, near, next_column, last_column] + others:
        pl.semaphore_signal(barrier, inc=1, device_id=to, device_id_type=pl.DeviceIdType.MESH)
    pl.semaphore_wait(barrier, 3 + owners)
    own_d.wait()
    own_x.wait()

    def pass_on(ref, send, recv, c):
        @pl.when((c <= column) & has_right)
        def _():
            remote(ref, send.at[0, c], recv.at[c], right).start()

        @pl.when((c >= column) & has_left)
        def _():
            remote(ref, send.at[1, c], recv.at[c], left).start()

    def passed(ref, send, recv, c):
        @pl.when((c <= column) & has_right)
        def _():
            remote(ref, send.at[0, c], recv.at[c], right).wait_send()

        @pl.when((c >= column) & has_left)
        def _():
            remote(ref, send.at[1, c], recv.at[c], left).wait_send()

    def at_distance(d, act):
        for c, there in ((column - d, column - d >= 0), (column + d, column + d < columns)):
            pl.when(there)(functools.partial(act, c))

    def spread(c):
        def act(i, ref):
            pass_on(ref, line_send.at[i], line_recv.at[i], c)
            remote(ref, far_send.at[i, c], far_recv.at[i, c], far).start()
            remote(ref, near_send.at[i, 0, c], near_recv.at[i, 0, c], near).start()

        cells(row, c, act)

    def arrived(c):
        def act(i, ref):
            remote(ref, line_send.at[i, 0, c], line_recv.at[i, c], right).wait_recv()

        cells(row, c, act)
        spread(c)

    def crossed(c):
        def act(i, ref):
            remote(ref, far_send.at[i, c], far_recv.at[i, c], far).wait_recv()
            remote(ref, near_send.at[i, 1, c], near_recv.at[i, 1, c], near).start()

        cells(far_row, c, act)

    def shared(c):
        def direct(i, ref):
            remote(ref, near_send.at[i, 0, c], near_recv.at[i, 0, c], near).wait_recv()

        def passed_on(i, ref):
            remote(ref, near_send.at[i, 1, c], near_recv.at[i, 1, c], near).wait_recv()

        cells(near_row, c, direct)
        cells(near_far_row, c, passed_on)

    def sent(c):
        def mine(i, ref):
            remote(ref, far_send.at[i, c], far_recv.at[i, c], far).wait_send()
            remote(ref, near_send.at[i, 0, c], near_recv.at[i, 0, c], near).wait_send()
            passed(ref, line_send.at[i], line_recv.at[i], c)

        def relayed(i, ref):
            remote(ref, near_send.at[i, 1, c], near_recv.at[i, 1, c], near).wait_send()

        cells(row, c, mine)
        cells(far_row, c, relayed)

    root = row == column
    relay = far_row == column
    from_near = jnp.logical_not(root | relay)

    def piece(ref, c, h):
        return ref.at[pl.ds(c * grains + h, 1)]

    def give(c, h):
        @pl.when(root)
        def _():
            for slot, to in ((0, far), (1, near)):
                pltpu.make_async_remote_copy(
                    src_ref=piece(br, c, h), dst_ref=piece(bc, c, h),
                    send_sem=c_send.at[h, slot, c], recv_sem=c_recv.at[h, c],
                    device_id=to, device_id_type=pl.DeviceIdType.MESH,
                ).start()

    def start_line():
        for h in range(grains):
            pass_on(piece(br, column, h), b_send.at[h], b_recv.at[h], column)

    def take(c):
        for h in range(grains):
            remote(piece(br, c, h), b_send.at[h, 0, c], b_recv.at[h, c], right).wait_recv()
            pass_on(piece(br, c, h), b_send.at[h], b_recv.at[h], c)
            give(c, h)

    def forward(c):
        @pl.when(relay)
        def _():
            for h in range(grains):
                remote(piece(bc, c, h), c_send.at[h, 0, c], c_recv.at[h, c], far).wait_recv()
                remote(piece(bc, c, h), c_send.at[h, 1, c], c_recv.at[h, c], near).start()

    spread(column)
    inside = has_left & has_right
    pl.when(jnp.logical_not(inside))(start_line)
    at_distance(1, arrived)
    crossed(column)
    for d in range(2, columns):
        at_distance(d, arrived)
        if d == max(columns - 2, 2):
            pl.when(inside)(start_line)
        at_distance(d - 1, crossed)
    at_distance(columns - 1, crossed)
    for h in range(grains):
        give(column, h)
    for c in range(columns):
        shared(c)
    for c in range(columns):
        sent(c)
    for i in range(n // 2, n, BLOCK):
        for j in range(0, n // 4, BLOCK):
            a[i : i + BLOCK, j : j + BLOCK] = a[j : j + BLOCK, i : i + BLOCK].T

    between = {}
    between[1] = [functools.partial(at_distance, 1, take)]
    between[2] = [functools.partial(forward, column)]
    between[4] = [functools.partial(at_distance, 1, forward)]
    between[5] = [functools.partial(at_distance, 2, take)]
    factor_in_place(a, w, lh, ll, between)
    factor_ref[...] = a[band(row, column), :]
    invert_diagonal(a, w, wh, wl)
    at_distance(2, forward)
    for d in range(3, columns - 1):
        at_distance(d, take)
        at_distance(d, forward)
    group = wh.shape[1]
    cut = group // 2

    def solve(i, carry):
        step = (i + 1) // 2
        inner = jnp.where(i % 2 == 1, column - step, column + step)
        outer = jnp.where(2 * column < columns, i, columns - 1 - i)
        c = jnp.where(i <= 2 * jnp.minimum(column, columns - 1 - column), inner, outer)
        at = pl.ds(c * grains, grains)
        if columns > 3:

            @pl.when(i == columns - 1)
            def _():
                at_distance(columns - 1, take)
                at_distance(columns - 1, forward)

        @pl.when(from_near)
        def _():
            for h in range(grains):
                remote(piece(bc, c, h), c_send.at[h, 0, c], c_recv.at[h, c], near).wait_recv()

        @pl.when(root)
        def _():
            bc[at] = br[at]

        for k in range(n // group):
            low, high = k * group, (k + 1) * group
            both = lambda y, x, cut: jnp.concatenate(
                [ref[at, :, cut].reshape(part, cut.stop - cut.start) for ref in (y, x)], axis=0
            )
            rest = both(br, bc, slice(low, high))
            if low:
                done = slice(0, low)
                rest = rest - split_dot(
                    (both(yh, xh, done), both(yl, xl, done)),
                    (lh[low:high, :low], ll[low:high, :low]),
                    NT,
                )
            rest = parts(rest)
            early = split_dot(
                tuple(z[:, :cut] for z in rest), (wh[k, :cut, :cut], wl[k, :cut, :cut]), NT
            )
            late = split_dot(rest, (wh[k, cut:, :], wl[k, cut:, :]), NT)
            for x, start in ((early, low), (late, low + cut)):
                stop = start + cut
                for (y_to, x_to), value in zip(((yh, xh), (yl, xl)), parts(x)):
                    y_to[at, :, start:stop] = value[:part].reshape(grains, grain, cut)
                    x_to[at, :, start:stop] = value[part:].reshape(grains, grain, cut)

                @pl.when(i == 0)
                def _(x=x, start=start, stop=stop):
                    panel_ref[:, start:stop] = x[:part]

        return carry

    lax.fori_loop(0, columns, solve, 0)
    own_t.wait()

    def owner(g, r, b):
        return (map_ref[g, r * blocks + b] % quarter) // per_owner

    mine = [owner(child, row, b) for b in range(blocks)]

    def pick(to, slot):
        block, rank = jnp.int32(0), jnp.int32(0)
        for b in range(blocks):
            here = mine[b] == to
            block = jnp.where(here & (rank == slot), b, block)
            rank += here.astype(jnp.int32)
        return block

    def give_away(s, d):
        return pltpu.make_async_remote_copy(
            src_ref=stage.at[s], dst_ref=piece_ref.at[blocks + s],
            send_sem=x_send.at[s], recv_sem=x_recv.at[s],
            device_id={"wide": lax.rem(child + d, owners)}, device_id_type=pl.DeviceIdType.MESH,
        )

    slots = [(d, i) for d in range(1, owners) for i in range(sure)]
    picked = [pick(lax.rem(child + d, owners), i) for d, i in slots]
    each = BLOCK // grain
    columns_side = tuple(x[...].reshape(q, n) for x in (xh, xl))
    for first in range(0, len(slots), 2):
        group = picked[first : first + 2]
        sides = tuple(
            jnp.concatenate([y[block * each + h] for block in group for h in range(each)], axis=0)
            for y in (yh, yl)
        )
        product = split_dot(sides, columns_side, NT)
        for e, block in enumerate(group):
            stage[first + e] = t[block] - product[e * BLOCK : e * BLOCK + BLOCK, :]
            give_away(first + e, slots[first + e][0]).start()
    step = 3 if blocks % 3 == 0 else 1
    for first in range(0, blocks, step):
        rows_side = tuple(
            y[first * each : (first + step) * each].reshape(step * BLOCK, n) for y in (yh, yl)
        )
        product = split_dot(rows_side, columns_side, NT)
        for e in range(step):
            piece_ref[first + e] = t[first + e] - product[e * BLOCK : e * BLOCK + BLOCK, :]
    for c in range(columns):
        for h in range(grains):

            @pl.when(relay)
            def _(c=c, h=h):
                remote(piece(bc, c, h), c_send.at[h, 1, c], c_recv.at[h, c], near).wait_send()

            @pl.when(root)
            def _(c=c, h=h):
                remote(piece(br, c, h), c_send.at[h, 0, c], c_recv.at[h, c], far).wait_send()
                remote(piece(br, c, h), c_send.at[h, 1, c], c_recv.at[h, c], near).wait_send()

            passed(piece(br, c, h), b_send.at[h], b_recv.at[h], c)
    need = jnp.int32(0)
    if sure < most_slots(blocks, per_owner):
        for g in range(owners):
            for r in range(rows):
                there = [owner(g, r, b) for b in range(blocks)]
                for e in range(owners):
                    if e != g:
                        need = jnp.maximum(need, sum((x == e).astype(jnp.int32) for x in there))
    need_ref[0] = need
    for s, (d, _) in enumerate(slots):
        give_away(s, d).wait()


def front_call(row_map, diag, lower, trailing, rows, columns, owners, sure, quarter):
    n = diag.shape[1]
    share, part = diag.shape[0], lower.shape[0]
    q = part * columns
    blocks = q // BLOCK
    dma = pltpu.SemaphoreType.DMA
    away = (owners - 1) * sure
    grain = math.gcd(part, BLOCK)
    grains = part // grain
    group = math.gcd(n, 4 * BLOCK)
    return pl.pallas_call(
        functools.partial(front_kernel, rows, columns, owners, sure, quarter),
        name="front",
        out_shape=(
            jax.ShapeDtypeStruct((share, n), F32),
            jax.ShapeDtypeStruct((part, n), F32),
            jax.ShapeDtypeStruct((blocks + away, BLOCK, q), F32),
            jax.ShapeDtypeStruct((1,), jnp.int32),
        ),
        in_specs=[SMEM] + [pl.BlockSpec(memory_space=pl.ANY)] * 3,
        out_specs=(VMEM,) * 3 + (SMEM,),
        scratch_shapes=[
            pltpu.VMEM((n, n), F32),
            pltpu.VMEM((n // BLOCK, BLOCK, BLOCK), F32),
            pltpu.VMEM((q // grain, grain, n), F32),
            pltpu.VMEM((q // grain, grain, n), F32),
            pltpu.VMEM((q // grain, grain, n), BF16),
            pltpu.VMEM((q // grain, grain, n), BF16),
            pltpu.VMEM((q // grain, grain, n), BF16),
            pltpu.VMEM((q // grain, grain, n), BF16),
            pltpu.VMEM((n, n), BF16),
            pltpu.VMEM((n, n), BF16),
            pltpu.VMEM((n // group, group, group), BF16),
            pltpu.VMEM((n // group, group, group), BF16),
            pltpu.VMEM((blocks, BLOCK, q), F32),
            pltpu.VMEM((away, BLOCK, q), F32),
            dma((away,)), dma((away,)),
            dma((3,)), dma((2, 2, columns)), dma((2, columns)), dma((2, columns)), dma((2, columns)),
            dma((2, 2, columns)), dma((2, 2, columns)),
            dma((grains, 2, columns)), dma((grains, columns)),
            dma((grains, 2, columns)), dma((grains, columns)),
        ],
        compiler_params=pltpu.CompilerParams(
            vmem_limit_bytes=56 << 20, collective_id=0, has_side_effects=True
        ),
    )(
        row_map, diag, lower.reshape(part // grain, grain, n), trailing.reshape(blocks, BLOCK, q)
    )


def rest_kernel(owners, sure, more, quarter, map_ref, piece_ref, out_ref, stage, send, recv):
    child, row = lax.axis_index("wide"), lax.axis_index("grow")
    blocks = out_ref.shape[2] // BLOCK
    per_owner = quarter // owners
    barrier = pltpu.get_barrier_semaphore()
    for d in range(1, owners):
        pl.semaphore_signal(
            barrier, inc=1, device_id={"wide": lax.rem(child + d, owners)},
            device_id_type=pl.DeviceIdType.MESH,
        )
    mine = [(map_ref[child, row * blocks + b] % quarter) // per_owner for b in range(blocks)]

    def give_away(s, d):
        return pltpu.make_async_remote_copy(
            src_ref=stage.at[s], dst_ref=out_ref.at[s], send_sem=send.at[s], recv_sem=recv.at[s],
            device_id={"wide": lax.rem(child + d, owners)}, device_id_type=pl.DeviceIdType.MESH,
        )

    slots = [(d, sure + i) for d in range(1, owners) for i in range(more)]
    for s, (d, slot) in enumerate(slots):
        block, rank = jnp.int32(0), jnp.int32(0)
        for b in range(blocks):
            here = mine[b] == lax.rem(child + d, owners)
            block = jnp.where(here & (rank == slot), b, block)
            rank += here.astype(jnp.int32)
        stage[s] = piece_ref[block]
    pl.semaphore_wait(barrier, owners - 1)
    for s, (d, _) in enumerate(slots):
        give_away(s, d).start()
    for s, (d, _) in enumerate(slots):
        give_away(s, d).wait()


def rest_call(row_map, pieces, owners, sure, more, quarter):
    away = (owners - 1) * more
    shape = (away,) + pieces.shape[1:]
    dma = pltpu.SemaphoreType.DMA
    return pl.pallas_call(
        functools.partial(rest_kernel, owners, sure, more, quarter),
        name="rest",
        out_shape=jax.ShapeDtypeStruct(shape, F32),
        in_specs=[SMEM, VMEM],
        out_specs=VMEM,
        scratch_shapes=[pltpu.VMEM(shape, F32), dma((away,)), dma((away,))],
        compiler_params=pltpu.CompilerParams(
            vmem_limit_bytes=12 << 20, collective_id=more, has_side_effects=True
        ),
    )(row_map, pieces)


def add_kernel(owners, sure, more, map_ref, parent_ref, factor_ref, panel_ref, *refs):
    pieces = refs[:-6]
    out_ref, factor_out, panel_out, total, read, write = refs[-6:]
    per_owner = total.shape[0] // BLOCK
    quarter = owners * per_owner
    q = pieces[0].shape[2]
    blocks = q // BLOCK
    column_blocks = total.shape[1] // BLOCK
    child, row = lax.axis_index("wide"), lax.axis_index("grow")
    column = lax.axis_index("gcol")

    def rows_of(p):
        return pl.ds(pl.multiple_of(p * BLOCK, BLOCK), BLOCK)

    def fetch(p):
        return pltpu.make_async_copy(parent_ref.at[rows_of(p)], total.at[rows_of(p)], read.at[p])

    def store(p):
        return pltpu.make_async_copy(total.at[rows_of(p)], out_ref.at[rows_of(p)], write.at[p])

    for p in range(per_owner):
        fetch(p).start()
    others = (
        pltpu.make_async_copy(factor_ref, factor_out, write.at[per_owner]),
        pltpu.make_async_copy(panel_ref, panel_out, write.at[per_owner + 1]),
    )

    def add_rows(p, carry):
        fetch(p).wait()

        def add(g, carry):
            block, slot, rank = jnp.int32(-1), jnp.int32(-1), jnp.int32(0)
            for b in range(blocks):
                to = map_ref[g, row * blocks + b] % quarter
                hit = to == child * per_owner + p
                block = jnp.where(hit, b, block)
                slot = jnp.where(hit, rank, slot)
                rank += (to // per_owner == child).astype(jnp.int32)
            away = lax.rem(child - g + owners, owners) - 1

            def put(ref, index):
                for b in range(blocks):
                    to = map_ref[g, column * blocks + b] % column_blocks
                    at = pl.ds(pl.multiple_of(to * BLOCK, BLOCK), BLOCK)
                    total[rows_of(p), at] += ref[index, :, b * BLOCK : b * BLOCK + BLOCK]

            @pl.when((block >= 0) & ((g == child) | (slot < sure)))
            def _():
                put(pieces[0], jnp.where(g == child, block, blocks + away * sure + slot))

            if len(pieces) > 1:

                @pl.when((block >= 0) & (g != child) & (slot >= sure))
                def _():
                    put(pieces[1], away * more + slot - sure)

            return carry

        lax.fori_loop(0, owners, add, 0)
        store(p).start()
        return carry

    lax.fori_loop(0, per_owner, add_rows, 0)
    for copy in others:
        copy.start()
    for p in range(per_owner):
        store(p).wait()
    for copy in others:
        copy.wait()


def add_call(row_map, parent, factor, panel, pieces, owners, sure, more):
    dma = pltpu.SemaphoreType.DMA
    per_owner = parent.shape[0] // BLOCK
    anywhere = pl.BlockSpec(memory_space=pl.ANY)
    return pl.pallas_call(
        functools.partial(add_kernel, owners, sure, more),
        name="extend_add",
        out_shape=tuple(jax.ShapeDtypeStruct(x.shape, F32) for x in (parent, factor, panel)),
        in_specs=[SMEM, anywhere] + [VMEM] * (2 + len(pieces)),
        out_specs=(anywhere,) * 3,
        scratch_shapes=[pltpu.VMEM(parent.shape, F32), dma((per_owner,)), dma((per_owner + 2,))],
        compiler_params=pltpu.CompilerParams(vmem_limit_bytes=24 << 20),
    )(row_map, parent, factor, panel, *pieces)


def body(diag_block, lower_block, trailing_block, parent_front, row_map):
    owners = lax.axis_size("wide")
    rows, columns = lax.axis_size("grow"), lax.axis_size("gcol")
    quarter = parent_front.shape[1] * owners // BLOCK
    blocks = trailing_block.shape[1] // BLOCK
    most = most_slots(blocks, quarter // owners)
    sure = max(1, 2 * most // 3)
    factor, panel, pieces, need = front_call(
        row_map, diag_block[0], lower_block[0], trailing_block[0], rows, columns, owners, sure, quarter,
    )

    def finish(more):
        def run():
            extra = (rest_call(row_map, pieces, owners, sure, more, quarter),) if more else ()
            return add_call(
                row_map, parent_front[0], factor, panel, (pieces,) + extra, owners, sure, more
            )

        return run

    branches = [finish(more) for more in range(most - sure + 1)]
    parent, factor, panel = lax.switch(jnp.clip(need[0] - sure, 0, most - sure), branches)
    return (factor[None], panel[None], parent[None])


def solution(mesh):
    placed = (
        P("wide", ("grow", "gcol"), None),
        P("wide", ("grow", "gcol"), None),
        P("wide", "grow", "gcol"),
        P("grow", "wide", "gcol"),
        P(),
    )
    return jax.shard_map(
        body,
        mesh=mesh,
        in_specs=placed,
        out_specs=(
            P("wide", ("grow", "gcol"), None),
            P("wide", ("grow", "gcol"), None),
            P("grow", "wide", "gcol"),
        ),
        check_vma=False,
    )
```

```python
import functools
import math

import jax
import jax.numpy as jnp
from jax import lax
from jax.experimental import pallas as pl
from jax.experimental.pallas import tpu as pltpu
from jax.sharding import PartitionSpec as P

BLOCK = 128
HALF = 64
F32 = jnp.float32
BF16 = jnp.bfloat16
NT = (((1,), (1,)), ((), ()))
NN = (((1,), (0,)), ((), ()))
VMEM = pl.BlockSpec(memory_space=pltpu.VMEM)
SMEM = pl.BlockSpec(memory_space=pltpu.SMEM)


def full_dot(a, b, dims):
    return lax.dot_general(
        a, b, dims, precision=lax.Precision.HIGHEST, preferred_element_type=F32
    )


def parts(x):
    high = x.astype(BF16)
    return high, (x - high.astype(F32)).astype(BF16)


def split_dot(a, b, dims):
    one = functools.partial(lax.dot_general, dimension_numbers=dims, preferred_element_type=F32)
    return one(a[0], b[0]) + (one(a[0], b[1]) + one(a[1], b[0]))


def factor_half(block):
    half = block.shape[0]
    rows = lax.broadcasted_iota(jnp.int32, (half, half), 0)
    cols = lax.broadcasted_iota(jnp.int32, (half, half), 1)
    eye = jnp.where(rows == cols, 1.0, 0.0).astype(F32)
    full = jnp.concatenate([block, eye], axis=1)
    count = half // 8
    wide = (8, 2 * half)
    groups = [full[8 * s : 8 * s + 8] for s in range(count)]
    sub = lax.broadcasted_iota(jnp.int32, wide, 0)
    at_row = [jnp.full(wide, i, jnp.int32) for i in range(8)]
    spread = lambda x: jnp.broadcast_to(x, wide)
    take = lambda x, i: jnp.take_along_axis(x, at_row[i], axis=0, mode="promise_in_bounds")
    done = []
    for s in range(count):
        c = 8 * s
        column = {
            t: [spread(groups[t][:, c + j : c + j + 1]) for j in range(8)] for t in range(s, count)
        }
        lead = [spread(groups[s][i : i + 1, :]) for i in range(8)]
        pivot = {(i, j): take(column[s][j], i) for i in range(8) for j in range(i, 8)}
        below = range(s + 1, count)
        keep = jnp.zeros(wide, F32)
        for j in range(8):
            r = lax.rsqrt(pivot[j, j])
            unit = lead[j] * r
            mult = {i: pivot[j, i] * r for i in range(j + 1, 8)}
            for i in range(j + 1, 8):
                for q in range(i, 8):
                    pivot[i, q] = pivot[i, q] - mult[i] * mult[q]
                lead[i] = lead[i] - mult[i] * unit
            for t in below:
                m = column[t][j] * r
                for i in range(j + 1, 8):
                    column[t][i] = column[t][i] - m * mult[i]
                groups[t] = groups[t] - m * unit
            keep = jnp.where(sub == j, unit, keep)
        done.append(keep)
    both = jnp.concatenate(done, axis=0)
    upper = jnp.where(rows <= cols, both[:, :half], 0.0)
    inverse = jnp.where(rows >= cols, both[:, half:], 0.0)
    return upper.T, inverse


def square(a, b, c):
    return jnp.concatenate(
        [
            jnp.concatenate([a, jnp.zeros_like(a)], axis=1),
            jnp.concatenate([b, c], axis=1),
        ],
        axis=0,
    )


def factor_in_place(a, w, lh, ll, between):
    n = a.shape[0]
    count = n // BLOCK

    def step(k, carry):
        o = pl.multiple_of(k * BLOCK, BLOCK)
        d = a[pl.ds(o, BLOCK), pl.ds(o, BLOCK)]
        l1, w1 = factor_half(d[:HALF, :HALF])
        l21 = full_dot(d[HALF:, :HALF], w1, NT)
        l2, w2 = factor_half(d[HALF:, HALF:] - full_dot(l21, l21, NT))
        w21 = -full_dot(w2, full_dot(l21, w1, NN), NN)
        a[pl.ds(o, BLOCK), pl.ds(o, BLOCK)] = square(l1, l21, l2)
        w[k] = square(w1, w21, w2)
        for at in range(count - 1):

            @pl.when(k == at)
            def _(at=at):
                low, high = at * BLOCK, at * BLOCK + BLOCK
                a[low:high, high:] = jnp.zeros((BLOCK, n - high), F32)
                p = split_dot(parts(a[high:, low:high]), parts(w[at]), NT)
                a[high:, low:high] = p
                lh[high:, low:high], ll[high:, low:high] = parts(p)
                end = min(high + (1 + at % 2) * BLOCK, n)
                start = 0 if at % 2 else low
                left, right = slice(high, n), slice(high, end)
                a[high:, high:end] = a[high:, high:end] - split_dot(
                    (lh[left, start:high], ll[left, start:high]),
                    (lh[right, start:high], ll[right, start:high]),
                    NT,
                )
                for act in between.get(at, ()):
                    act()

        return carry

    lax.fori_loop(0, count, step, 0)


def most_slots(blocks, per_owner):
    return min(blocks, per_owner)


def invert_diagonal(l_ref, w_ref, wh, wl):
    group = wh.shape[1]

    def inverse(at, size):
        if size == BLOCK:
            return w_ref[at // BLOCK]
        cut = size // 2
        first, second = inverse(at, cut), inverse(at + cut, cut)
        across = l_ref[at + cut : at + size, at : at + cut]
        product = parts(split_dot(parts(across), parts(first), NN))
        return square(first, -split_dot(parts(second), product, NN), second)

    for k in range(wh.shape[0]):
        wh[k], wl[k] = parts(inverse(k * group, group))


def front_kernel(
    rows, columns, owners, sure, quarter, map_ref, d_ref, x_ref, t_ref,
    factor_ref, panel_ref, piece_ref, need_ref,
    a, w, br, bc, xh, xl, yh, yl, lh, ll, wh, wl, t, stage, x_send, x_recv,
    local, line_send, line_recv, far_send, far_recv, near_send, near_recv,
    b_send, b_recv, c_send, c_recv,
):
    child = lax.axis_index("wide")
    row, column = lax.axis_index("grow"), lax.axis_index("gcol")
    n = a.shape[1]
    grain = br.shape[1]
    q = br.shape[0] * grain
    blocks = q // BLOCK
    per_owner = quarter // owners
    far_row = lax.rem(row + rows // 2, rows)
    near_row = row + 1 - 2 * lax.rem(row, 2)
    near_far_row = lax.rem(near_row + rows // 2, rows)
    right, left = {"gcol": column + 1}, {"gcol": column - 1}
    far, near = {"grow": far_row}, {"grow": near_row}
    share = d_ref.shape[0]
    grains = x_ref.shape[0]
    part = grains * grain
    has_left, has_right = column > 0, column < columns - 1

    def band(r, c):
        return pl.ds(pl.multiple_of((r * columns + c) * share, share), share)

    def cells(r, c, act):
        outer = (r == 0) | (r == rows - 1)
        start = jnp.where(outer, n // 2, jnp.where(r < rows // 2, 0, n // 4))
        act(0, a.at[band(r, c), pl.ds(pl.multiple_of(start, n // 4), n // 2)])
        extra = jnp.where(r == 0, 0, n // 4)
        slim = a.at[band(r, c), pl.ds(pl.multiple_of(extra, n // 4), n // 4)]
        pl.when(outer)(functools.partial(act, 1, slim))

    def remote(ref, send, recv, to):
        return pltpu.make_async_remote_copy(
            src_ref=ref, dst_ref=ref, send_sem=send, recv_sem=recv,
            device_id=to, device_id_type=pl.DeviceIdType.MESH,
        )

    own_d = pltpu.make_async_copy(d_ref, a.at[band(row, column)], local.at[0])
    own_x = pltpu.make_async_copy(x_ref, br.at[pl.ds(column * grains, grains)], local.at[1])
    own_t = pltpu.make_async_copy(t_ref, t, local.at[2])
    own_d.start()
    own_x.start()
    own_t.start()
    barrier = pltpu.get_barrier_semaphore()
    next_column = {"gcol": lax.rem(column + 1, columns)}
    last_column = {"gcol": lax.rem(column + columns - 1, columns)}
    others = [{"wide": lax.rem(child + d, owners)} for d in range(1, owners)]
    for to in [far, near, next_column, last_column] + others:
        pl.semaphore_signal(barrier, inc=1, device_id=to, device_id_type=pl.DeviceIdType.MESH)
    pl.semaphore_wait(barrier, 3 + owners)
    own_d.wait()
    own_x.wait()

    def pass_on(ref, send, recv, c):
        @pl.when((c <= column) & has_right)
        def _():
            remote(ref, send.at[0, c], recv.at[c], right).start()

        @pl.when((c >= column) & has_left)
        def _():
            remote(ref, send.at[1, c], recv.at[c], left).start()

    def passed(ref, send, recv, c):
        @pl.when((c <= column) & has_right)
        def _():
            remote(ref, send.at[0, c], recv.at[c], right).wait_send()

        @pl.when((c >= column) & has_left)
        def _():
            remote(ref, send.at[1, c], recv.at[c], left).wait_send()

    def at_distance(d, act):
        for c, there in ((column - d, column - d >= 0), (column + d, column + d < columns)):
            pl.when(there)(functools.partial(act, c))

    def spread(c):
        def act(i, ref):
            pass_on(ref, line_send.at[i], line_recv.at[i], c)
            remote(ref, far_send.at[i, c], far_recv.at[i, c], far).start()
            remote(ref, near_send.at[i, 0, c], near_recv.at[i, 0, c], near).start()

        cells(row, c, act)

    def arrived(c):
        def act(i, ref):
            remote(ref, line_send.at[i, 0, c], line_recv.at[i, c], right).wait_recv()

        cells(row, c, act)
        spread(c)

    def crossed(c):
        def act(i, ref):
            remote(ref, far_send.at[i, c], far_recv.at[i, c], far).wait_recv()
            remote(ref, near_send.at[i, 1, c], near_recv.at[i, 1, c], near).start()

        cells(far_row, c, act)

    def shared(c):
        def direct(i, ref):
            remote(ref, near_send.at[i, 0, c], near_recv.at[i, 0, c], near).wait_recv()

        def passed_on(i, ref):
            remote(ref, near_send.at[i, 1, c], near_recv.at[i, 1, c], near).wait_recv()

        cells(near_row, c, direct)
        cells(near_far_row, c, passed_on)

    def sent(c):
        def mine(i, ref):
            remote(ref, far_send.at[i, c], far_recv.at[i, c], far).wait_send()
            remote(ref, near_send.at[i, 0, c], near_recv.at[i, 0, c], near).wait_send()
            passed(ref, line_send.at[i], line_recv.at[i], c)

        def relayed(i, ref):
            remote(ref, near_send.at[i, 1, c], near_recv.at[i, 1, c], near).wait_send()

        cells(row, c, mine)
        cells(far_row, c, relayed)

    root = row == column
    relay = far_row == column
    from_near = jnp.logical_not(root | relay)

    def piece(ref, c, h):
        return ref.at[pl.ds(c * grains + h, 1)]

    def give(c, h):
        @pl.when(root)
        def _():
            for slot, to in ((0, far), (1, near)):
                pltpu.make_async_remote_copy(
                    src_ref=piece(br, c, h), dst_ref=piece(bc, c, h),
                    send_sem=c_send.at[h, slot, c], recv_sem=c_recv.at[h, c],
                    device_id=to, device_id_type=pl.DeviceIdType.MESH,
                ).start()

    def start_line():
        for h in range(grains):
            pass_on(piece(br, column, h), b_send.at[h], b_recv.at[h], column)

    def take(c, start=0, stop=3):
        for h in range(grains * start // 3, grains * stop // 3):
            remote(piece(br, c, h), b_send.at[h, 0, c], b_recv.at[h, c], right).wait_recv()
            pass_on(piece(br, c, h), b_send.at[h], b_recv.at[h], c)
            give(c, h)

    def forward(c, start=0, stop=3):
        @pl.when(relay)
        def _():
            for h in range(grains * start // 3, grains * stop // 3):
                remote(piece(bc, c, h), c_send.at[h, 0, c], c_recv.at[h, c], far).wait_recv()
                remote(piece(bc, c, h), c_send.at[h, 1, c], c_recv.at[h, c], near).start()

    spread(column)
    inside = has_left & has_right
    at_distance(1, arrived)
    crossed(column)
    for d in range(2, columns):
        at_distance(d, arrived)
        if d == max(columns - 2, 2):
            start_line()
        at_distance(d - 1, crossed)
    at_distance(columns - 1, crossed)
    for c in range(columns):
        shared(c)
    for c in range(columns):
        sent(c)
    for h in range(grains):
        give(column, h)
    for i in range(n // 2, n, BLOCK):
        for j in range(0, n // 4, BLOCK):
            a[i : i + BLOCK, j : j + BLOCK] = a[j : j + BLOCK, i : i + BLOCK].T

    between = {}
    some = lambda start, stop: functools.partial(take, start=start, stop=stop)
    between[1] = [functools.partial(at_distance, 1, take)]
    between[2] = [functools.partial(forward, column)]
    between[4] = [functools.partial(at_distance, 2, some(0, 2)), functools.partial(at_distance, 1, forward)]
    between[5] = [functools.partial(at_distance, 2, some(2, 3))]
    factor_in_place(a, w, lh, ll, between)
    factor_ref[...] = a[band(row, column), :]
    invert_diagonal(a, w, wh, wl)
    for d in range(3, columns - 1):
        at_distance(d, take)
        at_distance(d, forward)
    group = wh.shape[1]
    cut = group // 2

    def solve(i, carry):
        step = (i + 1) // 2
        inner = jnp.where(i % 2 == 1, column - step, column + step)
        outer = jnp.where(2 * column < columns, i, columns - 1 - i)
        c = jnp.where(i <= 2 * jnp.minimum(column, columns - 1 - column), inner, outer)
        at = pl.ds(c * grains, grains)
        def events(*acts):
            for d, act in acts:
                if d == 2 or d > 2 and d == columns - 1:
                    at_distance(d, act)

        some_on = lambda start, stop: functools.partial(forward, start=start, stop=stop)
        last = max(columns - 1, 3)
        pl.when(i == 0)(lambda: events((last, some(0, 1))))
        pl.when(i == 1)(lambda: events((2, forward), (last, some(1, 2))))
        pl.when(i == 2)(lambda: events((last, some(2, 3)), (last, some_on(0, 1))))
        pl.when(i == 3)(lambda: events((last, some_on(1, 3))))

        @pl.when(from_near)
        def _():
            for h in range(grains):
                remote(piece(bc, c, h), c_send.at[h, 0, c], c_recv.at[h, c], near).wait_recv()

        @pl.when(root)
        def _():
            bc[at] = br[at]

        for k in range(n // group):
            low, high = k * group, (k + 1) * group
            both = lambda y, x, cut: jnp.concatenate(
                [ref[at, :, cut].reshape(part, cut.stop - cut.start) for ref in (y, x)], axis=0
            )
            rest = both(br, bc, slice(low, high))
            if low:
                done = slice(0, low)
                rest = rest - split_dot(
                    (both(yh, xh, done), both(yl, xl, done)),
                    (lh[low:high, :low], ll[low:high, :low]),
                    NT,
                )
            rest = parts(rest)
            early = split_dot(
                tuple(z[:, :cut] for z in rest), (wh[k, :cut, :cut], wl[k, :cut, :cut]), NT
            )
            late = split_dot(rest, (wh[k, cut:, :], wl[k, cut:, :]), NT)
            for x, start in ((early, low), (late, low + cut)):
                stop = start + cut
                for (y_to, x_to), value in zip(((yh, xh), (yl, xl)), parts(x)):
                    y_to[at, :, start:stop] = value[:part].reshape(grains, grain, cut)
                    x_to[at, :, start:stop] = value[part:].reshape(grains, grain, cut)

                @pl.when(i == 0)
                def _(x=x, start=start, stop=stop):
                    panel_ref[:, start:stop] = x[:part]

        return carry

    lax.fori_loop(0, columns, solve, 0)
    own_t.wait()

    def owner(g, r, b):
        return (map_ref[g, r * blocks + b] % quarter) // per_owner

    mine = [owner(child, row, b) for b in range(blocks)]

    def pick(to, slot):
        block, rank = jnp.int32(0), jnp.int32(0)
        for b in range(blocks):
            here = mine[b] == to
            block = jnp.where(here & (rank == slot), b, block)
            rank += here.astype(jnp.int32)
        return block

    def give_away(s, d):
        return pltpu.make_async_remote_copy(
            src_ref=stage.at[s], dst_ref=piece_ref.at[blocks + s],
            send_sem=x_send.at[s], recv_sem=x_recv.at[s],
            device_id={"wide": lax.rem(child + d, owners)}, device_id_type=pl.DeviceIdType.MESH,
        )

    slots = [(d, i) for d in range(1, owners) for i in range(sure)]
    picked = [pick(lax.rem(child + d, owners), i) for d, i in slots]
    each = BLOCK // grain
    columns_side = tuple(x[...].reshape(q, n) for x in (xh, xl))
    for first in range(0, len(slots), 2):
        group = picked[first : first + 2]
        sides = tuple(
            jnp.concatenate([y[block * each + h] for block in group for h in range(each)], axis=0)
            for y in (yh, yl)
        )
        product = split_dot(sides, columns_side, NT)
        for e, block in enumerate(group):
            stage[first + e] = t[block] - product[e * BLOCK : e * BLOCK + BLOCK, :]
            give_away(first + e, slots[first + e][0]).start()
    step = 3 if blocks % 3 == 0 else 1
    for first in range(0, blocks, step):
        rows_side = tuple(
            y[first * each : (first + step) * each].reshape(step * BLOCK, n) for y in (yh, yl)
        )
        product = split_dot(rows_side, columns_side, NT)
        for e in range(step):
            piece_ref[first + e] = t[first + e] - product[e * BLOCK : e * BLOCK + BLOCK, :]
    for c in range(columns):
        for h in range(grains):

            @pl.when(relay)
            def _(c=c, h=h):
                remote(piece(bc, c, h), c_send.at[h, 1, c], c_recv.at[h, c], near).wait_send()

            @pl.when(root)
            def _(c=c, h=h):
                remote(piece(br, c, h), c_send.at[h, 0, c], c_recv.at[h, c], far).wait_send()
                remote(piece(br, c, h), c_send.at[h, 1, c], c_recv.at[h, c], near).wait_send()

            passed(piece(br, c, h), b_send.at[h], b_recv.at[h], c)
    need = jnp.int32(0)
    if sure < most_slots(blocks, per_owner):
        for g in range(owners):
            for r in range(rows):
                there = [owner(g, r, b) for b in range(blocks)]
                for e in range(owners):
                    if e != g:
                        need = jnp.maximum(need, sum((x == e).astype(jnp.int32) for x in there))
    need_ref[0] = need
    for s, (d, _) in enumerate(slots):
        give_away(s, d).wait()


def front_call(row_map, diag, lower, trailing, rows, columns, owners, sure, quarter):
    n = diag.shape[1]
    share, part = diag.shape[0], lower.shape[0]
    q = part * columns
    blocks = q // BLOCK
    dma = pltpu.SemaphoreType.DMA
    away = (owners - 1) * sure
    grain = math.gcd(part, BLOCK)
    grains = part // grain
    group = math.gcd(n, 4 * BLOCK)
    return pl.pallas_call(
        functools.partial(front_kernel, rows, columns, owners, sure, quarter),
        name="front",
        out_shape=(
            jax.ShapeDtypeStruct((share, n), F32),
            jax.ShapeDtypeStruct((part, n), F32),
            jax.ShapeDtypeStruct((blocks + away, BLOCK, q), F32),
            jax.ShapeDtypeStruct((1,), jnp.int32),
        ),
        in_specs=[SMEM] + [pl.BlockSpec(memory_space=pl.ANY)] * 3,
        out_specs=(VMEM,) * 3 + (SMEM,),
        scratch_shapes=[
            pltpu.VMEM((n, n), F32),
            pltpu.VMEM((n // BLOCK, BLOCK, BLOCK), F32),
            pltpu.VMEM((q // grain, grain, n), F32),
            pltpu.VMEM((q // grain, grain, n), F32),
            pltpu.VMEM((q // grain, grain, n), BF16),
            pltpu.VMEM((q // grain, grain, n), BF16),
            pltpu.VMEM((q // grain, grain, n), BF16),
            pltpu.VMEM((q // grain, grain, n), BF16),
            pltpu.VMEM((n, n), BF16),
            pltpu.VMEM((n, n), BF16),
            pltpu.VMEM((n // group, group, group), BF16),
            pltpu.VMEM((n // group, group, group), BF16),
            pltpu.VMEM((blocks, BLOCK, q), F32),
            pltpu.VMEM((away, BLOCK, q), F32),
            dma((away,)), dma((away,)),
            dma((3,)), dma((2, 2, columns)), dma((2, columns)), dma((2, columns)), dma((2, columns)),
            dma((2, 2, columns)), dma((2, 2, columns)),
            dma((grains, 2, columns)), dma((grains, columns)),
            dma((grains, 2, columns)), dma((grains, columns)),
        ],
        compiler_params=pltpu.CompilerParams(
            vmem_limit_bytes=56 << 20, collective_id=0, has_side_effects=True
        ),
    )(
        row_map, diag, lower.reshape(part // grain, grain, n), trailing.reshape(blocks, BLOCK, q)
    )


def rest_kernel(owners, sure, more, quarter, map_ref, piece_ref, out_ref, stage, send, recv):
    child, row = lax.axis_index("wide"), lax.axis_index("grow")
    blocks = out_ref.shape[2] // BLOCK
    per_owner = quarter // owners
    barrier = pltpu.get_barrier_semaphore()
    for d in range(1, owners):
        pl.semaphore_signal(
            barrier, inc=1, device_id={"wide": lax.rem(child + d, owners)},
            device_id_type=pl.DeviceIdType.MESH,
        )
    mine = [(map_ref[child, row * blocks + b] % quarter) // per_owner for b in range(blocks)]

    def give_away(s, d):
        return pltpu.make_async_remote_copy(
            src_ref=stage.at[s], dst_ref=out_ref.at[s], send_sem=send.at[s], recv_sem=recv.at[s],
            device_id={"wide": lax.rem(child + d, owners)}, device_id_type=pl.DeviceIdType.MESH,
        )

    slots = [(d, sure + i) for d in range(1, owners) for i in range(more)]
    for s, (d, slot) in enumerate(slots):
        block, rank = jnp.int32(0), jnp.int32(0)
        for b in range(blocks):
            here = mine[b] == lax.rem(child + d, owners)
            block = jnp.where(here & (rank == slot), b, block)
            rank += here.astype(jnp.int32)
        stage[s] = piece_ref[block]
    pl.semaphore_wait(barrier, owners - 1)
    for s, (d, _) in enumerate(slots):
        give_away(s, d).start()
    for s, (d, _) in enumerate(slots):
        give_away(s, d).wait()


def rest_call(row_map, pieces, owners, sure, more, quarter):
    away = (owners - 1) * more
    shape = (away,) + pieces.shape[1:]
    dma = pltpu.SemaphoreType.DMA
    return pl.pallas_call(
        functools.partial(rest_kernel, owners, sure, more, quarter),
        name="rest",
        out_shape=jax.ShapeDtypeStruct(shape, F32),
        in_specs=[SMEM, VMEM],
        out_specs=VMEM,
        scratch_shapes=[pltpu.VMEM(shape, F32), dma((away,)), dma((away,))],
        compiler_params=pltpu.CompilerParams(
            vmem_limit_bytes=12 << 20, collective_id=more, has_side_effects=True
        ),
    )(row_map, pieces)


def add_kernel(owners, sure, more, map_ref, parent_ref, factor_ref, panel_ref, *refs):
    pieces = refs[:-6]
    out_ref, factor_out, panel_out, total, read, write = refs[-6:]
    per_owner = total.shape[0] // BLOCK
    quarter = owners * per_owner
    q = pieces[0].shape[2]
    blocks = q // BLOCK
    column_blocks = total.shape[1] // BLOCK
    child, row = lax.axis_index("wide"), lax.axis_index("grow")
    column = lax.axis_index("gcol")

    def rows_of(p):
        return pl.ds(pl.multiple_of(p * BLOCK, BLOCK), BLOCK)

    def fetch(p):
        return pltpu.make_async_copy(parent_ref.at[rows_of(p)], total.at[rows_of(p)], read.at[p])

    def store(p):
        return pltpu.make_async_copy(total.at[rows_of(p)], out_ref.at[rows_of(p)], write.at[p])

    for p in range(per_owner):
        fetch(p).start()
    others = (
        pltpu.make_async_copy(factor_ref, factor_out, write.at[per_owner]),
        pltpu.make_async_copy(panel_ref, panel_out, write.at[per_owner + 1]),
    )

    def add_rows(p, carry):
        fetch(p).wait()

        def add(g, carry):
            block, slot, rank = jnp.int32(-1), jnp.int32(-1), jnp.int32(0)
            for b in range(blocks):
                to = map_ref[g, row * blocks + b] % quarter
                hit = to == child * per_owner + p
                block = jnp.where(hit, b, block)
                slot = jnp.where(hit, rank, slot)
                rank += (to // per_owner == child).astype(jnp.int32)
            away = lax.rem(child - g + owners, owners) - 1

            def put(ref, index):
                for b in range(blocks):
                    to = map_ref[g, column * blocks + b] % column_blocks
                    at = pl.ds(pl.multiple_of(to * BLOCK, BLOCK), BLOCK)
                    total[rows_of(p), at] += ref[index, :, b * BLOCK : b * BLOCK + BLOCK]

            @pl.when((block >= 0) & ((g == child) | (slot < sure)))
            def _():
                put(pieces[0], jnp.where(g == child, block, blocks + away * sure + slot))

            if len(pieces) > 1:

                @pl.when((block >= 0) & (g != child) & (slot >= sure))
                def _():
                    put(pieces[1], away * more + slot - sure)

            return carry

        lax.fori_loop(0, owners, add, 0)
        store(p).start()
        return carry

    lax.fori_loop(0, per_owner, add_rows, 0)
    for copy in others:
        copy.start()
    for p in range(per_owner):
        store(p).wait()
    for copy in others:
        copy.wait()


def add_call(row_map, parent, factor, panel, pieces, owners, sure, more):
    dma = pltpu.SemaphoreType.DMA
    per_owner = parent.shape[0] // BLOCK
    anywhere = pl.BlockSpec(memory_space=pl.ANY)
    return pl.pallas_call(
        functools.partial(add_kernel, owners, sure, more),
        name="extend_add",
        out_shape=tuple(jax.ShapeDtypeStruct(x.shape, F32) for x in (parent, factor, panel)),
        in_specs=[SMEM, anywhere] + [VMEM] * (2 + len(pieces)),
        out_specs=(anywhere,) * 3,
        scratch_shapes=[pltpu.VMEM(parent.shape, F32), dma((per_owner,)), dma((per_owner + 2,))],
        compiler_params=pltpu.CompilerParams(vmem_limit_bytes=24 << 20),
    )(row_map, parent, factor, panel, *pieces)


def body(diag_block, lower_block, trailing_block, parent_front, row_map):
    owners = lax.axis_size("wide")
    rows, columns = lax.axis_size("grow"), lax.axis_size("gcol")
    quarter = parent_front.shape[1] * owners // BLOCK
    blocks = trailing_block.shape[1] // BLOCK
    most = most_slots(blocks, quarter // owners)
    sure = max(1, 2 * most // 3)
    factor, panel, pieces, need = front_call(
        row_map, diag_block[0], lower_block[0], trailing_block[0], rows, columns, owners, sure, quarter,
    )

    def finish(more):
        def run():
            extra = (rest_call(row_map, pieces, owners, sure, more, quarter),) if more else ()
            return add_call(
                row_map, parent_front[0], factor, panel, (pieces,) + extra, owners, sure, more
            )

        return run

    branches = [finish(more) for more in range(most - sure + 1)]
    parent, factor, panel = lax.switch(jnp.clip(need[0] - sure, 0, most - sure), branches)
    return (factor[None], panel[None], parent[None])


def solution(mesh):
    placed = (
        P("wide", ("grow", "gcol"), None),
        P("wide", ("grow", "gcol"), None),
        P("wide", "grow", "gcol"),
        P("grow", "wide", "gcol"),
        P(),
    )
    return jax.shard_map(
        body,
        mesh=mesh,
        in_specs=placed,
        out_specs=(
            P("wide", ("grow", "gcol"), None),
            P("wide", ("grow", "gcol"), None),
            P("grow", "wide", "gcol"),
        ),
        check_vma=False,
    )
```

```python
import functools
import math

import jax
import jax.numpy as jnp
from jax import lax
from jax.experimental import pallas as pl
from jax.experimental.pallas import tpu as pltpu
from jax.sharding import PartitionSpec as P

BLOCK = 128
HALF = 64
F32 = jnp.float32
BF16 = jnp.bfloat16
NT = (((1,), (1,)), ((), ()))
NN = (((1,), (0,)), ((), ()))
VMEM = pl.BlockSpec(memory_space=pltpu.VMEM)
SMEM = pl.BlockSpec(memory_space=pltpu.SMEM)


def full_dot(a, b, dims):
    return lax.dot_general(
        a, b, dims, precision=lax.Precision.HIGHEST, preferred_element_type=F32
    )


def parts(x):
    high = x.astype(BF16)
    return high, (x - high.astype(F32)).astype(BF16)


def split_dot(a, b, dims):
    one = functools.partial(lax.dot_general, dimension_numbers=dims, preferred_element_type=F32)
    return one(a[0], b[0]) + (one(a[0], b[1]) + one(a[1], b[0]))


def factor_half(block):
    half = block.shape[0]
    rows = lax.broadcasted_iota(jnp.int32, (half, half), 0)
    cols = lax.broadcasted_iota(jnp.int32, (half, half), 1)
    eye = jnp.where(rows == cols, 1.0, 0.0).astype(F32)
    full = jnp.concatenate([block, eye], axis=1)
    count = half // 8
    wide = (8, 2 * half)
    groups = [full[8 * s : 8 * s + 8] for s in range(count)]
    sub = lax.broadcasted_iota(jnp.int32, wide, 0)
    at_row = [jnp.full(wide, i, jnp.int32) for i in range(8)]
    spread = lambda x: jnp.broadcast_to(x, wide)
    take = lambda x, i: jnp.take_along_axis(x, at_row[i], axis=0, mode="promise_in_bounds")
    done = []
    for s in range(count):
        c = 8 * s
        column = {
            t: [spread(groups[t][:, c + j : c + j + 1]) for j in range(8)] for t in range(s, count)
        }
        lead = [spread(groups[s][i : i + 1, :]) for i in range(8)]
        pivot = {(i, j): take(column[s][j], i) for i in range(8) for j in range(i, 8)}
        below = range(s + 1, count)
        keep = jnp.zeros(wide, F32)
        for j in range(8):
            r = lax.rsqrt(pivot[j, j])
            unit = lead[j] * r
            mult = {i: pivot[j, i] * r for i in range(j + 1, 8)}
            for i in range(j + 1, 8):
                for q in range(i, 8):
                    pivot[i, q] = pivot[i, q] - mult[i] * mult[q]
                lead[i] = lead[i] - mult[i] * unit
            for t in below:
                m = column[t][j] * r
                for i in range(j + 1, 8):
                    column[t][i] = column[t][i] - m * mult[i]
                groups[t] = groups[t] - m * unit
            keep = jnp.where(sub == j, unit, keep)
        done.append(keep)
    both = jnp.concatenate(done, axis=0)
    upper = jnp.where(rows <= cols, both[:, :half], 0.0)
    inverse = jnp.where(rows >= cols, both[:, half:], 0.0)
    return upper.T, inverse


def square(a, b, c):
    return jnp.concatenate(
        [
            jnp.concatenate([a, jnp.zeros_like(a)], axis=1),
            jnp.concatenate([b, c], axis=1),
        ],
        axis=0,
    )


def factor_in_place(a, w, lh, ll, between):
    n = a.shape[0]
    count = n // BLOCK

    def step(k, carry):
        o = pl.multiple_of(k * BLOCK, BLOCK)
        d = a[pl.ds(o, BLOCK), pl.ds(o, BLOCK)]
        l1, w1 = factor_half(d[:HALF, :HALF])
        l21 = full_dot(d[HALF:, :HALF], w1, NT)
        l2, w2 = factor_half(d[HALF:, HALF:] - full_dot(l21, l21, NT))
        w21 = -full_dot(w2, full_dot(l21, w1, NN), NN)
        a[pl.ds(o, BLOCK), pl.ds(o, BLOCK)] = square(l1, l21, l2)
        w[k] = square(w1, w21, w2)
        for at in range(count - 1):

            @pl.when(k == at)
            def _(at=at):
                low, high = at * BLOCK, at * BLOCK + BLOCK
                a[low:high, high:] = jnp.zeros((BLOCK, n - high), F32)
                p = split_dot(parts(a[high:, low:high]), parts(w[at]), NT)
                a[high:, low:high] = p
                lh[high:, low:high], ll[high:, low:high] = parts(p)
                end = min(high + (1 + at % 2) * BLOCK, n)
                start = 0 if at % 2 else low
                left, right = slice(high, n), slice(high, end)
                a[high:, high:end] = a[high:, high:end] - split_dot(
                    (lh[left, start:high], ll[left, start:high]),
                    (lh[right, start:high], ll[right, start:high]),
                    NT,
                )
                for act in between.get(at, ()):
                    act()

        return carry

    lax.fori_loop(0, count, step, 0)


def most_slots(blocks, per_owner):
    return min(blocks, per_owner)


def invert_diagonal(l_ref, w_ref, wh, wl):
    group = wh.shape[1]

    def inverse(at, size):
        if size == BLOCK:
            return w_ref[at // BLOCK]
        cut = size // 2
        first, second = inverse(at, cut), inverse(at + cut, cut)
        across = l_ref[at + cut : at + size, at : at + cut]
        product = parts(split_dot(parts(across), parts(first), NN))
        return square(first, -split_dot(parts(second), product, NN), second)

    for k in range(wh.shape[0]):
        wh[k], wl[k] = parts(inverse(k * group, group))


def front_kernel(
    rows, columns, owners, sure, quarter, map_ref, d_ref, x_ref, t_ref, parent_ref,
    factor_ref, panel_ref, piece_ref, held_ref, need_ref,
    a, w, br, bc, xh, xl, yh, yl, lh, ll, wh, wl, t, stage, x_send, x_recv,
    local, line_send, line_recv, far_send, far_recv, near_send, near_recv,
    b_send, b_recv, c_send, c_recv,
):
    child = lax.axis_index("wide")
    row, column = lax.axis_index("grow"), lax.axis_index("gcol")
    n = a.shape[1]
    grain = br.shape[1]
    q = br.shape[0] * grain
    blocks = q // BLOCK
    per_owner = quarter // owners
    far_row = lax.rem(row + rows // 2, rows)
    near_row = row + 1 - 2 * lax.rem(row, 2)
    near_far_row = lax.rem(near_row + rows // 2, rows)
    right, left = {"gcol": column + 1}, {"gcol": column - 1}
    far, near = {"grow": far_row}, {"grow": near_row}
    share = d_ref.shape[0]
    grains = x_ref.shape[0]
    part = grains * grain
    has_left, has_right = column > 0, column < columns - 1

    def band(r, c):
        return pl.ds(pl.multiple_of((r * columns + c) * share, share), share)

    def cells(r, c, act):
        outer = (r == 0) | (r == rows - 1)
        start = jnp.where(outer, n // 2, jnp.where(r < rows // 2, 0, n // 4))
        act(0, a.at[band(r, c), pl.ds(pl.multiple_of(start, n // 4), n // 2)])
        extra = jnp.where(r == 0, 0, n // 4)
        slim = a.at[band(r, c), pl.ds(pl.multiple_of(extra, n // 4), n // 4)]
        pl.when(outer)(functools.partial(act, 1, slim))

    def remote(ref, send, recv, to):
        return pltpu.make_async_remote_copy(
            src_ref=ref, dst_ref=ref, send_sem=send, recv_sem=recv,
            device_id=to, device_id_type=pl.DeviceIdType.MESH,
        )

    own_d = pltpu.make_async_copy(d_ref, a.at[band(row, column)], local.at[0])
    own_x = pltpu.make_async_copy(x_ref, br.at[pl.ds(column * grains, grains)], local.at[1])
    own_t = pltpu.make_async_copy(t_ref, t, local.at[2])
    own_d.start()
    own_x.start()
    own_t.start()
    own_p = pltpu.make_async_copy(parent_ref, held_ref, local.at[3])
    barrier = pltpu.get_barrier_semaphore()
    next_column = {"gcol": lax.rem(column + 1, columns)}
    last_column = {"gcol": lax.rem(column + columns - 1, columns)}
    others = [{"wide": lax.rem(child + d, owners)} for d in range(1, owners)]
    for to in [far, near, next_column, last_column] + others:
        pl.semaphore_signal(barrier, inc=1, device_id=to, device_id_type=pl.DeviceIdType.MESH)
    pl.semaphore_wait(barrier, 3 + owners)
    own_d.wait()
    own_x.wait()
    own_p.start()

    def pass_on(ref, send, recv, c):
        @pl.when((c <= column) & has_right)
        def _():
            remote(ref, send.at[0, c], recv.at[c], right).start()

        @pl.when((c >= column) & has_left)
        def _():
            remote(ref, send.at[1, c], recv.at[c], left).start()

    def passed(ref, send, recv, c):
        @pl.when((c <= column) & has_right)
        def _():
            remote(ref, send.at[0, c], recv.at[c], right).wait_send()

        @pl.when((c >= column) & has_left)
        def _():
            remote(ref, send.at[1, c], recv.at[c], left).wait_send()

    def at_distance(d, act):
        for c, there in ((column - d, column - d >= 0), (column + d, column + d < columns)):
            pl.when(there)(functools.partial(act, c))

    def spread(c):
        def act(i, ref):
            pass_on(ref, line_send.at[i], line_recv.at[i], c)
            remote(ref, far_send.at[i, c], far_recv.at[i, c], far).start()
            remote(ref, near_send.at[i, 0, c], near_recv.at[i, 0, c], near).start()

        cells(row, c, act)

    def arrived(c):
        def act(i, ref):
            remote(ref, line_send.at[i, 0, c], line_recv.at[i, c], right).wait_recv()

        cells(row, c, act)
        spread(c)

    def crossed(c):
        def act(i, ref):
            remote(ref, far_send.at[i, c], far_recv.at[i, c], far).wait_recv()
            remote(ref, near_send.at[i, 1, c], near_recv.at[i, 1, c], near).start()

        cells(far_row, c, act)

    def shared(c):
        def direct(i, ref):
            remote(ref, near_send.at[i, 0, c], near_recv.at[i, 0, c], near).wait_recv()

        def passed_on(i, ref):
            remote(ref, near_send.at[i, 1, c], near_recv.at[i, 1, c], near).wait_recv()

        cells(near_row, c, direct)
        cells(near_far_row, c, passed_on)

    def sent(c):
        def mine(i, ref):
            remote(ref, far_send.at[i, c], far_recv.at[i, c], far).wait_send()
            remote(ref, near_send.at[i, 0, c], near_recv.at[i, 0, c], near).wait_send()
            passed(ref, line_send.at[i], line_recv.at[i], c)

        def relayed(i, ref):
            remote(ref, near_send.at[i, 1, c], near_recv.at[i, 1, c], near).wait_send()

        cells(row, c, mine)
        cells(far_row, c, relayed)

    root = row == column
    relay = far_row == column
    from_near = jnp.logical_not(root | relay)

    def piece(ref, c, h):
        return ref.at[pl.ds(c * grains + h, 1)]

    def give(c, h):
        @pl.when(root)
        def _():
            for slot, to in ((0, far), (1, near)):
                pltpu.make_async_remote_copy(
                    src_ref=piece(br, c, h), dst_ref=piece(bc, c, h),
                    send_sem=c_send.at[h, slot, c], recv_sem=c_recv.at[h, c],
                    device_id=to, device_id_type=pl.DeviceIdType.MESH,
                ).start()

    def start_line():
        for h in range(grains):
            pass_on(piece(br, column, h), b_send.at[h], b_recv.at[h], column)

    def take(c, start=0, stop=3):
        for h in range(grains * start // 3, grains * stop // 3):
            remote(piece(br, c, h), b_send.at[h, 0, c], b_recv.at[h, c], right).wait_recv()
            pass_on(piece(br, c, h), b_send.at[h], b_recv.at[h], c)
            give(c, h)

    def forward(c, start=0, stop=3):
        @pl.when(relay)
        def _():
            for h in range(grains * start // 3, grains * stop // 3):
                remote(piece(bc, c, h), c_send.at[h, 0, c], c_recv.at[h, c], far).wait_recv()
                remote(piece(bc, c, h), c_send.at[h, 1, c], c_recv.at[h, c], near).start()

    spread(column)
    inside = has_left & has_right
    at_distance(1, arrived)
    crossed(column)
    for d in range(2, columns):
        at_distance(d, arrived)
        if d == max(columns - 2, 2):
            start_line()
        at_distance(d - 1, crossed)
    at_distance(columns - 1, crossed)
    for c in range(columns):
        shared(c)
    for c in range(columns):
        sent(c)
    for h in range(grains):
        give(column, h)
    for i in range(n // 2, n, BLOCK):
        for j in range(0, n // 4, BLOCK):
            a[i : i + BLOCK, j : j + BLOCK] = a[j : j + BLOCK, i : i + BLOCK].T

    between = {}
    some = lambda start, stop: functools.partial(take, start=start, stop=stop)
    between[1] = [functools.partial(at_distance, 1, take)]
    between[2] = [functools.partial(forward, column)]
    between[4] = [functools.partial(at_distance, 2, some(0, 2)), functools.partial(at_distance, 1, forward)]
    between[5] = [functools.partial(at_distance, 2, some(2, 3))]
    factor_in_place(a, w, lh, ll, between)
    factor_ref[...] = a[band(row, column), :]
    invert_diagonal(a, w, wh, wl)
    for d in range(3, columns - 1):
        at_distance(d, take)
        at_distance(d, forward)
    group = wh.shape[1]
    cut = group // 2

    def solve(i, carry):
        step = (i + 1) // 2
        inner = jnp.where(i % 2 == 1, column - step, column + step)
        outer = jnp.where(2 * column < columns, i, columns - 1 - i)
        c = jnp.where(i <= 2 * jnp.minimum(column, columns - 1 - column), inner, outer)
        at = pl.ds(c * grains, grains)
        def events(*acts):
            for d, act in acts:
                if d == 2 or d > 2 and d == columns - 1:
                    at_distance(d, act)

        some_on = lambda start, stop: functools.partial(forward, start=start, stop=stop)
        last = max(columns - 1, 3)
        pl.when(i == 0)(lambda: events((last, some(0, 1))))
        pl.when(i == 1)(lambda: events((2, forward), (last, some(1, 2))))
        pl.when(i == 2)(lambda: events((last, some(2, 3)), (last, some_on(0, 1))))
        pl.when(i == 3)(lambda: events((last, some_on(1, 3))))

        @pl.when(from_near)
        def _():
            for h in range(grains):
                remote(piece(bc, c, h), c_send.at[h, 0, c], c_recv.at[h, c], near).wait_recv()

        @pl.when(root)
        def _():
            bc[at] = br[at]

        for k in range(n // group):
            low, high = k * group, (k + 1) * group
            both = lambda y, x, cut: jnp.concatenate(
                [ref[at, :, cut].reshape(part, cut.stop - cut.start) for ref in (y, x)], axis=0
            )
            rest = both(br, bc, slice(low, high))
            if low:
                done = slice(0, low)
                rest = rest - split_dot(
                    (both(yh, xh, done), both(yl, xl, done)),
                    (lh[low:high, :low], ll[low:high, :low]),
                    NT,
                )
            rest = parts(rest)
            early = split_dot(
                tuple(z[:, :cut] for z in rest), (wh[k, :cut, :cut], wl[k, :cut, :cut]), NT
            )
            late = split_dot(rest, (wh[k, cut:, :], wl[k, cut:, :]), NT)
            for x, start in ((early, low), (late, low + cut)):
                stop = start + cut
                for (y_to, x_to), value in zip(((yh, xh), (yl, xl)), parts(x)):
                    y_to[at, :, start:stop] = value[:part].reshape(grains, grain, cut)
                    x_to[at, :, start:stop] = value[part:].reshape(grains, grain, cut)

                @pl.when(i == 0)
                def _(x=x, start=start, stop=stop):
                    panel_ref[:, start:stop] = x[:part]

        return carry

    lax.fori_loop(0, columns, solve, 0)
    own_t.wait()

    def owner(g, r, b):
        return (map_ref[g, r * blocks + b] % quarter) // per_owner

    mine = [owner(child, row, b) for b in range(blocks)]

    def pick(to, slot):
        block, rank = jnp.int32(0), jnp.int32(0)
        for b in range(blocks):
            here = mine[b] == to
            block = jnp.where(here & (rank == slot), b, block)
            rank += here.astype(jnp.int32)
        return block

    def give_away(s, d):
        return pltpu.make_async_remote_copy(
            src_ref=stage.at[s], dst_ref=piece_ref.at[blocks + s],
            send_sem=x_send.at[s], recv_sem=x_recv.at[s],
            device_id={"wide": lax.rem(child + d, owners)}, device_id_type=pl.DeviceIdType.MESH,
        )

    slots = [(d, i) for d in range(1, owners) for i in range(sure)]
    picked = [pick(lax.rem(child + d, owners), i) for d, i in slots]
    each = BLOCK // grain
    columns_side = tuple(x[...].reshape(q, n) for x in (xh, xl))
    for first in range(0, len(slots), 2):
        group = picked[first : first + 2]
        sides = tuple(
            jnp.concatenate([y[block * each + h] for block in group for h in range(each)], axis=0)
            for y in (yh, yl)
        )
        product = split_dot(sides, columns_side, NT)
        for e, block in enumerate(group):
            stage[first + e] = t[block] - product[e * BLOCK : e * BLOCK + BLOCK, :]
            give_away(first + e, slots[first + e][0]).start()
    step = 3 if blocks % 3 == 0 else 1
    for first in range(0, blocks, step):
        rows_side = tuple(
            y[first * each : (first + step) * each].reshape(step * BLOCK, n) for y in (yh, yl)
        )
        product = split_dot(rows_side, columns_side, NT)
        for e in range(step):
            piece_ref[first + e] = t[first + e] - product[e * BLOCK : e * BLOCK + BLOCK, :]
    for c in range(columns):
        for h in range(grains):

            @pl.when(relay)
            def _(c=c, h=h):
                remote(piece(bc, c, h), c_send.at[h, 1, c], c_recv.at[h, c], near).wait_send()

            @pl.when(root)
            def _(c=c, h=h):
                remote(piece(br, c, h), c_send.at[h, 0, c], c_recv.at[h, c], far).wait_send()
                remote(piece(br, c, h), c_send.at[h, 1, c], c_recv.at[h, c], near).wait_send()

            passed(piece(br, c, h), b_send.at[h], b_recv.at[h], c)
    need = jnp.int32(0)
    if sure < most_slots(blocks, per_owner):
        for g in range(owners):
            for r in range(rows):
                there = [owner(g, r, b) for b in range(blocks)]
                for e in range(owners):
                    if e != g:
                        need = jnp.maximum(need, sum((x == e).astype(jnp.int32) for x in there))
    need_ref[0] = need
    own_p.wait()
    for s, (d, _) in enumerate(slots):
        give_away(s, d).wait()


def front_call(row_map, diag, lower, trailing, parent, rows, columns, owners, sure, quarter):
    n = diag.shape[1]
    share, part = diag.shape[0], lower.shape[0]
    q = part * columns
    blocks = q // BLOCK
    dma = pltpu.SemaphoreType.DMA
    away = (owners - 1) * sure
    grain = math.gcd(part, BLOCK)
    grains = part // grain
    group = math.gcd(n, 4 * BLOCK)
    arrays = (
        diag, lower.reshape(part // grain, grain, n), trailing.reshape(blocks, BLOCK, q), parent
    )
    return pl.pallas_call(
        functools.partial(front_kernel, rows, columns, owners, sure, quarter),
        name="front",
        out_shape=(
            jax.ShapeDtypeStruct((share, n), F32),
            jax.ShapeDtypeStruct((part, n), F32),
            jax.ShapeDtypeStruct((blocks + away, BLOCK, q), F32),
            jax.ShapeDtypeStruct(parent.shape, F32),
            jax.ShapeDtypeStruct((1,), jnp.int32),
        ),
        in_specs=[SMEM] + [pl.BlockSpec(memory_space=pltpu.HBM)] * 4,
        out_specs=(VMEM,) * 4 + (SMEM,),
        scratch_shapes=[
            pltpu.VMEM((n, n), F32),
            pltpu.VMEM((n // BLOCK, BLOCK, BLOCK), F32),
            pltpu.VMEM((q // grain, grain, n), F32),
            pltpu.VMEM((q // grain, grain, n), F32),
            pltpu.VMEM((q // grain, grain, n), BF16),
            pltpu.VMEM((q // grain, grain, n), BF16),
            pltpu.VMEM((q // grain, grain, n), BF16),
            pltpu.VMEM((q // grain, grain, n), BF16),
            pltpu.VMEM((n, n), BF16),
            pltpu.VMEM((n, n), BF16),
            pltpu.VMEM((n // group, group, group), BF16),
            pltpu.VMEM((n // group, group, group), BF16),
            pltpu.VMEM((blocks, BLOCK, q), F32),
            pltpu.VMEM((away, BLOCK, q), F32),
            dma((away,)), dma((away,)),
            dma((4,)), dma((2, 2, columns)), dma((2, columns)), dma((2, columns)), dma((2, columns)),
            dma((2, 2, columns)), dma((2, 2, columns)),
            dma((grains, 2, columns)), dma((grains, columns)),
            dma((grains, 2, columns)), dma((grains, columns)),
        ],
        compiler_params=pltpu.CompilerParams(
            vmem_limit_bytes=40 << 20, collective_id=0, has_side_effects=True
        ),
    )(row_map, *(pltpu.with_memory_space_constraint(x, pltpu.HBM) for x in arrays))


def rest_kernel(owners, sure, more, quarter, map_ref, piece_ref, out_ref, stage, send, recv):
    child, row = lax.axis_index("wide"), lax.axis_index("grow")
    blocks = out_ref.shape[2] // BLOCK
    per_owner = quarter // owners
    barrier = pltpu.get_barrier_semaphore()
    for d in range(1, owners):
        pl.semaphore_signal(
            barrier, inc=1, device_id={"wide": lax.rem(child + d, owners)},
            device_id_type=pl.DeviceIdType.MESH,
        )
    mine = [(map_ref[child, row * blocks + b] % quarter) // per_owner for b in range(blocks)]

    def give_away(s, d):
        return pltpu.make_async_remote_copy(
            src_ref=stage.at[s], dst_ref=out_ref.at[s], send_sem=send.at[s], recv_sem=recv.at[s],
            device_id={"wide": lax.rem(child + d, owners)}, device_id_type=pl.DeviceIdType.MESH,
        )

    slots = [(d, sure + i) for d in range(1, owners) for i in range(more)]
    for s, (d, slot) in enumerate(slots):
        block, rank = jnp.int32(0), jnp.int32(0)
        for b in range(blocks):
            here = mine[b] == lax.rem(child + d, owners)
            block = jnp.where(here & (rank == slot), b, block)
            rank += here.astype(jnp.int32)
        stage[s] = piece_ref[block]
    pl.semaphore_wait(barrier, owners - 1)
    for s, (d, _) in enumerate(slots):
        give_away(s, d).start()
    for s, (d, _) in enumerate(slots):
        give_away(s, d).wait()


def rest_call(row_map, pieces, owners, sure, more, quarter):
    away = (owners - 1) * more
    shape = (away,) + pieces.shape[1:]
    dma = pltpu.SemaphoreType.DMA
    return pl.pallas_call(
        functools.partial(rest_kernel, owners, sure, more, quarter),
        name="rest",
        out_shape=jax.ShapeDtypeStruct(shape, F32),
        in_specs=[SMEM, VMEM],
        out_specs=VMEM,
        scratch_shapes=[pltpu.VMEM(shape, F32), dma((away,)), dma((away,))],
        compiler_params=pltpu.CompilerParams(
            vmem_limit_bytes=12 << 20, collective_id=more, has_side_effects=True
        ),
    )(row_map, pieces)


def add_kernel(owners, sure, more, map_ref, parent_ref, factor_ref, panel_ref, *refs):
    pieces = refs[:-5]
    out_ref, factor_out, panel_out, total, write = refs[-5:]
    per_owner = total.shape[0] // BLOCK
    quarter = owners * per_owner
    q = pieces[0].shape[2]
    blocks = q // BLOCK
    column_blocks = total.shape[1] // BLOCK
    child, row = lax.axis_index("wide"), lax.axis_index("grow")
    column = lax.axis_index("gcol")

    def rows_of(p):
        return pl.ds(pl.multiple_of(p * BLOCK, BLOCK), BLOCK)

    def store(p):
        return pltpu.make_async_copy(total.at[rows_of(p)], out_ref.at[rows_of(p)], write.at[p])

    others = (
        pltpu.make_async_copy(factor_ref, factor_out, write.at[per_owner]),
        pltpu.make_async_copy(panel_ref, panel_out, write.at[per_owner + 1]),
    )

    def add_rows(p, carry):
        total[rows_of(p), :] = parent_ref[rows_of(p), :]

        def add(g, carry):
            block, slot, rank = jnp.int32(-1), jnp.int32(-1), jnp.int32(0)
            for b in range(blocks):
                to = map_ref[g, row * blocks + b] % quarter
                hit = to == child * per_owner + p
                block = jnp.where(hit, b, block)
                slot = jnp.where(hit, rank, slot)
                rank += (to // per_owner == child).astype(jnp.int32)
            away = lax.rem(child - g + owners, owners) - 1

            def put(ref, index):
                for b in range(blocks):
                    to = map_ref[g, column * blocks + b] % column_blocks
                    at = pl.ds(pl.multiple_of(to * BLOCK, BLOCK), BLOCK)
                    total[rows_of(p), at] += ref[index, :, b * BLOCK : b * BLOCK + BLOCK]

            @pl.when((block >= 0) & ((g == child) | (slot < sure)))
            def _():
                put(pieces[0], jnp.where(g == child, block, blocks + away * sure + slot))

            if len(pieces) > 1:

                @pl.when((block >= 0) & (g != child) & (slot >= sure))
                def _():
                    put(pieces[1], away * more + slot - sure)

            return carry

        lax.fori_loop(0, owners, add, 0)
        store(p).start()
        return carry

    lax.fori_loop(0, per_owner, add_rows, 0)
    for copy in others:
        copy.start()
    for p in range(per_owner):
        store(p).wait()
    for copy in others:
        copy.wait()


def add_call(row_map, parent, factor, panel, pieces, owners, sure, more):
    dma = pltpu.SemaphoreType.DMA
    per_owner = parent.shape[0] // BLOCK
    anywhere = pl.BlockSpec(memory_space=pl.ANY)
    return pl.pallas_call(
        functools.partial(add_kernel, owners, sure, more),
        name="extend_add",
        out_shape=tuple(jax.ShapeDtypeStruct(x.shape, F32) for x in (parent, factor, panel)),
        in_specs=[SMEM] + [VMEM] * (3 + len(pieces)),
        out_specs=(anywhere,) * 3,
        scratch_shapes=[pltpu.VMEM(parent.shape, F32), dma((per_owner + 2,))],
        compiler_params=pltpu.CompilerParams(vmem_limit_bytes=24 << 20),
    )(row_map, parent, factor, panel, *pieces)


def body(diag_block, lower_block, trailing_block, parent_front, row_map):
    owners = lax.axis_size("wide")
    rows, columns = lax.axis_size("grow"), lax.axis_size("gcol")
    quarter = parent_front.shape[1] * owners // BLOCK
    blocks = trailing_block.shape[1] // BLOCK
    most = most_slots(blocks, quarter // owners)
    sure = max(1, 2 * most // 3)
    factor, panel, pieces, held, need = front_call(
        row_map, diag_block[0], lower_block[0], trailing_block[0], parent_front[0],
        rows, columns, owners, sure, quarter,
    )

    def finish(more):
        def run():
            extra = (rest_call(row_map, pieces, owners, sure, more, quarter),) if more else ()
            return add_call(
                row_map, held, factor, panel, (pieces,) + extra, owners, sure, more
            )

        return run

    branches = [finish(more) for more in range(most - sure + 1)]
    parent, factor, panel = lax.switch(jnp.clip(need[0] - sure, 0, most - sure), branches)
    return (factor[None], panel[None], parent[None])


def solution(mesh):
    placed = (
        P("wide", ("grow", "gcol"), None),
        P("wide", ("grow", "gcol"), None),
        P("wide", "grow", "gcol"),
        P("grow", "wide", "gcol"),
        P(),
    )
    return jax.shard_map(
        body,
        mesh=mesh,
        in_specs=placed,
        out_specs=(
            P("wide", ("grow", "gcol"), None),
            P("wide", ("grow", "gcol"), None),
            P("grow", "wide", "gcol"),
        ),
        check_vma=False,
    )
```

```python
import functools
import math

import jax
import jax.numpy as jnp
from jax import lax
from jax.experimental import pallas as pl
from jax.experimental.pallas import tpu as pltpu
from jax.sharding import PartitionSpec as P

BLOCK = 128
HALF = 64
F32 = jnp.float32
BF16 = jnp.bfloat16
NT = (((1,), (1,)), ((), ()))
NN = (((1,), (0,)), ((), ()))
VMEM = pl.BlockSpec(memory_space=pltpu.VMEM)
SMEM = pl.BlockSpec(memory_space=pltpu.SMEM)


def full_dot(a, b, dims):
    return lax.dot_general(
        a, b, dims, precision=lax.Precision.HIGHEST, preferred_element_type=F32
    )


def parts(x):
    high = x.astype(BF16)
    return high, (x - high.astype(F32)).astype(BF16)


def split_dot(a, b, dims):
    one = functools.partial(lax.dot_general, dimension_numbers=dims, preferred_element_type=F32)
    return one(a[0], b[0]) + (one(a[0], b[1]) + one(a[1], b[0]))


def factor_half(block):
    half = block.shape[0]
    rows = lax.broadcasted_iota(jnp.int32, (half, half), 0)
    cols = lax.broadcasted_iota(jnp.int32, (half, half), 1)
    eye = jnp.where(rows == cols, 1.0, 0.0).astype(F32)
    full = jnp.concatenate([block, eye], axis=1)
    count = half // 8
    wide = (8, 2 * half)
    groups = [full[8 * s : 8 * s + 8] for s in range(count)]
    sub = lax.broadcasted_iota(jnp.int32, wide, 0)
    at_row = [jnp.full(wide, i, jnp.int32) for i in range(8)]
    spread = lambda x: jnp.broadcast_to(x, wide)
    take = lambda x, i: jnp.take_along_axis(x, at_row[i], axis=0, mode="promise_in_bounds")
    done = []
    for s in range(count):
        c = 8 * s
        column = {
            t: [spread(groups[t][:, c + j : c + j + 1]) for j in range(8)] for t in range(s, count)
        }
        lead = [spread(groups[s][i : i + 1, :]) for i in range(8)]
        pivot = {(i, j): take(column[s][j], i) for i in range(8) for j in range(i, 8)}
        below = range(s + 1, count)
        keep = jnp.zeros(wide, F32)
        for j in range(8):
            r = lax.rsqrt(pivot[j, j])
            unit = lead[j] * r
            mult = {i: pivot[j, i] * r for i in range(j + 1, 8)}
            for i in range(j + 1, 8):
                for q in range(i, 8):
                    pivot[i, q] = pivot[i, q] - mult[i] * mult[q]
                lead[i] = lead[i] - mult[i] * unit
            for t in below:
                m = column[t][j] * r
                for i in range(j + 1, 8):
                    column[t][i] = column[t][i] - m * mult[i]
                groups[t] = groups[t] - m * unit
            keep = jnp.where(sub == j, unit, keep)
        done.append(keep)
    both = jnp.concatenate(done, axis=0)
    upper = jnp.where(rows <= cols, both[:, :half], 0.0)
    inverse = jnp.where(rows >= cols, both[:, half:], 0.0)
    return upper.T, inverse


def square(a, b, c):
    return jnp.concatenate(
        [
            jnp.concatenate([a, jnp.zeros_like(a)], axis=1),
            jnp.concatenate([b, c], axis=1),
        ],
        axis=0,
    )


def factor_in_place(a, w, lh, ll, between):
    n = a.shape[0]
    count = n // BLOCK

    def step(k, carry):
        o = pl.multiple_of(k * BLOCK, BLOCK)
        d = a[pl.ds(o, BLOCK), pl.ds(o, BLOCK)]
        l1, w1 = factor_half(d[:HALF, :HALF])
        l21 = full_dot(d[HALF:, :HALF], w1, NT)
        l2, w2 = factor_half(d[HALF:, HALF:] - full_dot(l21, l21, NT))
        w21 = -full_dot(w2, full_dot(l21, w1, NN), NN)
        a[pl.ds(o, BLOCK), pl.ds(o, BLOCK)] = square(l1, l21, l2)
        w[k] = square(w1, w21, w2)
        for at in range(count - 1):

            @pl.when(k == at)
            def _(at=at):
                low, high = at * BLOCK, at * BLOCK + BLOCK
                a[low:high, high:] = jnp.zeros((BLOCK, n - high), F32)
                p = split_dot(parts(a[high:, low:high]), parts(w[at]), NT)
                a[high:, low:high] = p
                lh[high:, low:high], ll[high:, low:high] = parts(p)
                end = min(high + (1 + at % 2) * BLOCK, n)
                start = 0 if at % 2 else low
                left, right = slice(high, n), slice(high, end)
                a[high:, high:end] = a[high:, high:end] - split_dot(
                    (lh[left, start:high], ll[left, start:high]),
                    (lh[right, start:high], ll[right, start:high]),
                    NT,
                )
                for act in between.get(at, ()):
                    act()

        return carry

    lax.fori_loop(0, count, step, 0)


def most_slots(blocks, per_owner):
    return min(blocks, per_owner)


def lends(owners, sure, most, rows):
    return owners == 2 and sure == 4 and sure < most <= sure + 2 and rows % 2 == 0


def invert_diagonal(l_ref, w_ref, wh, wl):
    group = wh.shape[1]

    def inverse(at, size):
        if size == BLOCK:
            return w_ref[at // BLOCK]
        cut = size // 2
        first, second = inverse(at, cut), inverse(at + cut, cut)
        across = l_ref[at + cut : at + size, at : at + cut]
        product = parts(split_dot(parts(across), parts(first), NN))
        return square(first, -split_dot(parts(second), product, NN), second)

    for k in range(wh.shape[0]):
        wh[k], wl[k] = parts(inverse(k * group, group))


def front_kernel(
    rows, columns, owners, sure, quarter, map_ref, d_ref, x_ref, t_ref, parent_ref,
    factor_ref, panel_ref, piece_ref, held_ref, need_ref,
    a, w, br, bc, xh, xl, yh, yl, lh, ll, wh, wl, t, stage, cand, lent, x_send, x_recv,
    o_send, o_recv, f_send, f_recv, local, line_send, line_recv, far_send, far_recv, near_send, near_recv,
    b_send, b_recv, c_send, c_recv,
):
    child = lax.axis_index("wide")
    row, column = lax.axis_index("grow"), lax.axis_index("gcol")
    n = a.shape[1]
    grain = br.shape[1]
    q = br.shape[0] * grain
    blocks = q // BLOCK
    per_owner = quarter // owners
    far_row = lax.rem(row + rows // 2, rows)
    near_row = row + 1 - 2 * lax.rem(row, 2)
    near_far_row = lax.rem(near_row + rows // 2, rows)
    right, left = {"gcol": column + 1}, {"gcol": column - 1}
    far, near = {"grow": far_row}, {"grow": near_row}
    share = d_ref.shape[0]
    grains = x_ref.shape[0]
    part = grains * grain
    has_left, has_right = column > 0, column < columns - 1

    def band(r, c):
        return pl.ds(pl.multiple_of((r * columns + c) * share, share), share)

    def cells(r, c, act):
        outer = (r == 0) | (r == rows - 1)
        start = jnp.where(outer, n // 2, jnp.where(r < rows // 2, 0, n // 4))
        act(0, a.at[band(r, c), pl.ds(pl.multiple_of(start, n // 4), n // 2)])
        extra = jnp.where(r == 0, 0, n // 4)
        slim = a.at[band(r, c), pl.ds(pl.multiple_of(extra, n // 4), n // 4)]
        pl.when(outer)(functools.partial(act, 1, slim))

    def remote(ref, send, recv, to):
        return pltpu.make_async_remote_copy(
            src_ref=ref, dst_ref=ref, send_sem=send, recv_sem=recv,
            device_id=to, device_id_type=pl.DeviceIdType.MESH,
        )

    own_d = pltpu.make_async_copy(d_ref, a.at[band(row, column)], local.at[0])
    own_x = pltpu.make_async_copy(x_ref, br.at[pl.ds(column * grains, grains)], local.at[1])
    own_t = pltpu.make_async_copy(t_ref, t, local.at[2])
    own_d.start()
    own_x.start()
    own_t.start()
    own_p = pltpu.make_async_copy(parent_ref, held_ref, local.at[3])
    barrier = pltpu.get_barrier_semaphore()
    next_column = {"gcol": lax.rem(column + 1, columns)}
    last_column = {"gcol": lax.rem(column + columns - 1, columns)}
    others = [{"wide": lax.rem(child + d, owners)} for d in range(1, owners)]
    for to in [far, near, next_column, last_column] + others:
        pl.semaphore_signal(barrier, inc=1, device_id=to, device_id_type=pl.DeviceIdType.MESH)
    pl.semaphore_wait(barrier, 3 + owners)
    own_d.wait()
    own_x.wait()
    own_p.start()

    def pass_on(ref, send, recv, c):
        @pl.when((c <= column) & has_right)
        def _():
            remote(ref, send.at[0, c], recv.at[c], right).start()

        @pl.when((c >= column) & has_left)
        def _():
            remote(ref, send.at[1, c], recv.at[c], left).start()

    def passed(ref, send, recv, c):
        @pl.when((c <= column) & has_right)
        def _():
            remote(ref, send.at[0, c], recv.at[c], right).wait_send()

        @pl.when((c >= column) & has_left)
        def _():
            remote(ref, send.at[1, c], recv.at[c], left).wait_send()

    def at_distance(d, act):
        for c, there in ((column - d, column - d >= 0), (column + d, column + d < columns)):
            pl.when(there)(functools.partial(act, c))

    def spread(c):
        def act(i, ref):
            pass_on(ref, line_send.at[i], line_recv.at[i], c)
            remote(ref, far_send.at[i, c], far_recv.at[i, c], far).start()
            remote(ref, near_send.at[i, 0, c], near_recv.at[i, 0, c], near).start()

        cells(row, c, act)

    def arrived(c):
        def act(i, ref):
            remote(ref, line_send.at[i, 0, c], line_recv.at[i, c], right).wait_recv()

        cells(row, c, act)
        spread(c)

    def crossed(c):
        def act(i, ref):
            remote(ref, far_send.at[i, c], far_recv.at[i, c], far).wait_recv()
            remote(ref, near_send.at[i, 1, c], near_recv.at[i, 1, c], near).start()

        cells(far_row, c, act)

    def shared(c):
        def direct(i, ref):
            remote(ref, near_send.at[i, 0, c], near_recv.at[i, 0, c], near).wait_recv()

        def passed_on(i, ref):
            remote(ref, near_send.at[i, 1, c], near_recv.at[i, 1, c], near).wait_recv()

        cells(near_row, c, direct)
        cells(near_far_row, c, passed_on)

    def sent(c):
        def mine(i, ref):
            remote(ref, far_send.at[i, c], far_recv.at[i, c], far).wait_send()
            remote(ref, near_send.at[i, 0, c], near_recv.at[i, 0, c], near).wait_send()
            passed(ref, line_send.at[i], line_recv.at[i], c)

        def relayed(i, ref):
            remote(ref, near_send.at[i, 1, c], near_recv.at[i, 1, c], near).wait_send()

        cells(row, c, mine)
        cells(far_row, c, relayed)

    root = row == column
    relay = far_row == column
    from_near = jnp.logical_not(root | relay)

    def piece(ref, c, h):
        return ref.at[pl.ds(c * grains + h, 1)]

    def give(c, h):
        @pl.when(root)
        def _():
            for slot, to in ((0, far), (1, near)):
                pltpu.make_async_remote_copy(
                    src_ref=piece(br, c, h), dst_ref=piece(bc, c, h),
                    send_sem=c_send.at[h, slot, c], recv_sem=c_recv.at[h, c],
                    device_id=to, device_id_type=pl.DeviceIdType.MESH,
                ).start()

    def start_line():
        for h in range(grains):
            pass_on(piece(br, column, h), b_send.at[h], b_recv.at[h], column)

    def take(c, start=0, stop=3):
        for h in range(grains * start // 3, grains * stop // 3):
            remote(piece(br, c, h), b_send.at[h, 0, c], b_recv.at[h, c], right).wait_recv()
            pass_on(piece(br, c, h), b_send.at[h], b_recv.at[h], c)
            give(c, h)

    def forward(c, start=0, stop=3):
        @pl.when(relay)
        def _():
            for h in range(grains * start // 3, grains * stop // 3):
                remote(piece(bc, c, h), c_send.at[h, 0, c], c_recv.at[h, c], far).wait_recv()
                remote(piece(bc, c, h), c_send.at[h, 1, c], c_recv.at[h, c], near).start()

    spread(column)
    inside = has_left & has_right
    at_distance(1, arrived)
    crossed(column)
    for d in range(2, columns):
        at_distance(d, arrived)
        if d == max(columns - 2, 2):
            start_line()
        at_distance(d - 1, crossed)
    at_distance(columns - 1, crossed)
    for c in range(columns):
        shared(c)
    for c in range(columns):
        sent(c)
    for h in range(grains):
        give(column, h)
    for i in range(n // 2, n, BLOCK):
        for j in range(0, n // 4, BLOCK):
            a[i : i + BLOCK, j : j + BLOCK] = a[j : j + BLOCK, i : i + BLOCK].T

    between = {}
    some = lambda start, stop: functools.partial(take, start=start, stop=stop)
    between[1] = [functools.partial(at_distance, 1, take)]
    between[2] = [functools.partial(forward, column)]
    between[4] = [functools.partial(at_distance, 2, some(0, 2)), functools.partial(at_distance, 1, forward)]
    between[5] = [functools.partial(at_distance, 2, some(2, 3))]
    factor_in_place(a, w, lh, ll, between)
    factor_ref[...] = a[band(row, column), :]
    invert_diagonal(a, w, wh, wl)
    for d in range(3, columns - 1):
        at_distance(d, take)
        at_distance(d, forward)
    group = wh.shape[1]
    cut = group // 2

    def solve(i, carry):
        step = (i + 1) // 2
        inner = jnp.where(i % 2 == 1, column - step, column + step)
        outer = jnp.where(2 * column < columns, i, columns - 1 - i)
        c = jnp.where(i <= 2 * jnp.minimum(column, columns - 1 - column), inner, outer)
        at = pl.ds(c * grains, grains)
        def events(*acts):
            for d, act in acts:
                if d == 2 or d > 2 and d == columns - 1:
                    at_distance(d, act)

        some_on = lambda start, stop: functools.partial(forward, start=start, stop=stop)
        last = max(columns - 1, 3)
        pl.when(i == 0)(lambda: events((last, some(0, 1))))
        pl.when(i == 1)(lambda: events((2, forward), (last, some(1, 2))))
        pl.when(i == 2)(lambda: events((last, some(2, 3)), (last, some_on(0, 1))))
        pl.when(i == 3)(lambda: events((last, some_on(1, 3))))

        @pl.when(from_near)
        def _():
            for h in range(grains):
                remote(piece(bc, c, h), c_send.at[h, 0, c], c_recv.at[h, c], near).wait_recv()

        @pl.when(root)
        def _():
            bc[at] = br[at]

        for k in range(n // group):
            low, high = k * group, (k + 1) * group
            both = lambda y, x, cut: jnp.concatenate(
                [ref[at, :, cut].reshape(part, cut.stop - cut.start) for ref in (y, x)], axis=0
            )
            rest = both(br, bc, slice(low, high))
            if low:
                done = slice(0, low)
                rest = rest - split_dot(
                    (both(yh, xh, done), both(yl, xl, done)),
                    (lh[low:high, :low], ll[low:high, :low]),
                    NT,
                )
            rest = parts(rest)
            early = split_dot(
                tuple(z[:, :cut] for z in rest), (wh[k, :cut, :cut], wl[k, :cut, :cut]), NT
            )
            late = split_dot(rest, (wh[k, cut:, :], wl[k, cut:, :]), NT)
            for x, start in ((early, low), (late, low + cut)):
                stop = start + cut
                for (y_to, x_to), value in zip(((yh, xh), (yl, xl)), parts(x)):
                    y_to[at, :, start:stop] = value[:part].reshape(grains, grain, cut)
                    x_to[at, :, start:stop] = value[part:].reshape(grains, grain, cut)

                @pl.when(i == 0)
                def _(x=x, start=start, stop=stop):
                    panel_ref[:, start:stop] = x[:part]

        return carry

    lax.fori_loop(0, columns, solve, 0)
    own_t.wait()

    def owner(g, r, b):
        return (map_ref[g, r * blocks + b] % quarter) // per_owner

    mine = [owner(child, row, b) for b in range(blocks)]

    def pick(to, slot):
        block, rank = jnp.int32(0), jnp.int32(0)
        for b in range(blocks):
            here = mine[b] == to
            block = jnp.where(here & (rank == slot), b, block)
            rank += here.astype(jnp.int32)
        return block

    def give_away(s, d):
        return pltpu.make_async_remote_copy(
            src_ref=stage.at[s], dst_ref=piece_ref.at[blocks + s],
            send_sem=x_send.at[s], recv_sem=x_recv.at[s],
            device_id={"wide": lax.rem(child + d, owners)}, device_id_type=pl.DeviceIdType.MESH,
        )

    slots = [(d, i) for d in range(1, owners) for i in range(sure)]
    lend = lends(owners, sure, most_slots(blocks, per_owner), rows)
    rank_at = (0, 2, 3, 1) if lend else tuple(range(sure))
    picked = [pick(lax.rem(child + d, owners), rank_at[i]) for d, i in slots]
    each = BLOCK // grain
    columns_side = tuple(x[...].reshape(q, n) for x in (xh, xl))

    def moved(group):
        sides = tuple(
            jnp.concatenate([y[block * each + h] for block in group for h in range(each)], axis=0)
            for y in (yh, yl)
        )
        product = split_dot(sides, columns_side, NT)
        return [t[b] - product[e * BLOCK : e * BLOCK + BLOCK, :] for e, b in enumerate(group)]

    def lend_on(o):
        return pltpu.make_async_remote_copy(
            src_ref=lent.at[o], dst_ref=cand.at[2 * o + 1], send_sem=o_send.at[o],
            recv_sem=o_recv.at[o], device_id=near, device_id_type=pl.DeviceIdType.MESH,
        )

    def hand_back(o):
        return pltpu.make_async_remote_copy(
            src_ref=piece_ref.at[blocks + 2 - o], dst_ref=piece_ref.at[blocks + sure + o],
            send_sem=f_send.at[o], recv_sem=f_recv.at[o], device_id=near,
            device_id_type=pl.DeviceIdType.MESH,
        )

    if lend:
        to = lax.rem(child + 1, owners)
        count = sum((x == to).astype(jnp.int32) for x in mine)
        stage[0], lent[0] = moved([picked[0], pick(to, sure)])
        give_away(0, 1).start()
        lend_on(0).start()
        lent[1], cand[2] = moved([pick(to, sure + 1), picked[1]])
        lend_on(1).start()
        cand[0], stage[3] = moved([picked[2], picked[3]])
        for o in range(2):
            lend_on(o).wait()
        for o in range(2):
            stage[2 - o] = cand[2 * o + jnp.where(count > 3 - o, 0, 1)]
        for s in (1, 2, 3):
            give_away(s, 1).start()
    else:
        for first in range(0, len(slots), 2):
            for e, value in enumerate(moved(picked[first : first + 2])):
                stage[first + e] = value
                give_away(first + e, slots[first + e][0]).start()
    step = 3 if blocks % 3 == 0 else 1
    for first in range(0, blocks, step):
        rows_side = tuple(
            y[first * each : (first + step) * each].reshape(step * BLOCK, n) for y in (yh, yl)
        )
        product = split_dot(rows_side, columns_side, NT)
        for e in range(step):
            piece_ref[first + e] = t[first + e] - product[e * BLOCK : e * BLOCK + BLOCK, :]
    for c in range(columns):
        for h in range(grains):

            @pl.when(relay)
            def _(c=c, h=h):
                remote(piece(bc, c, h), c_send.at[h, 1, c], c_recv.at[h, c], near).wait_send()

            @pl.when(root)
            def _(c=c, h=h):
                remote(piece(br, c, h), c_send.at[h, 0, c], c_recv.at[h, c], far).wait_send()
                remote(piece(br, c, h), c_send.at[h, 1, c], c_recv.at[h, c], near).wait_send()

            passed(piece(br, c, h), b_send.at[h], b_recv.at[h], c)
    need = jnp.int32(0)
    if sure < most_slots(blocks, per_owner):
        for g in range(owners):
            counts = [
                [
                    sum((x == e).astype(jnp.int32) for x in there)
                    for e in range(owners)
                    if e != g
                ]
                for there in ([owner(g, r, b) for b in range(blocks)] for r in range(rows))
            ]
            for r in range(rows):
                for e, k in enumerate(counts[r]):
                    if lend:
                        beside = counts[r + 1 - 2 * (r % 2)][e]
                        stuck = (k > sure) & (beside > 3) | (k > sure + 1) & (beside > 2)
                        k = jnp.where(stuck, k, 0)
                    need = jnp.maximum(need, k)
    need_ref[0] = need
    own_p.wait()
    if lend:
        for o in (1, 0):
            give_away(2 - o, 1).wait_recv()
            hand_back(o).start()
    for s, (d, _) in enumerate(slots):
        if lend and s in (1, 2):
            give_away(s, d).wait_send()
        else:
            give_away(s, d).wait()
    if lend:
        for o in range(2):
            hand_back(o).wait()


def front_call(row_map, diag, lower, trailing, parent, rows, columns, owners, sure, quarter):
    n = diag.shape[1]
    share, part = diag.shape[0], lower.shape[0]
    q = part * columns
    blocks = q // BLOCK
    dma = pltpu.SemaphoreType.DMA
    away = (owners - 1) * sure
    grain = math.gcd(part, BLOCK)
    grains = part // grain
    group = math.gcd(n, 4 * BLOCK)
    most = most_slots(blocks, quarter // owners)
    extra = 2 if lends(owners, sure, most, rows) else 0
    arrays = (
        diag, lower.reshape(part // grain, grain, n), trailing.reshape(blocks, BLOCK, q), parent
    )
    return pl.pallas_call(
        functools.partial(front_kernel, rows, columns, owners, sure, quarter),
        name="front",
        out_shape=(
            jax.ShapeDtypeStruct((share, n), F32),
            jax.ShapeDtypeStruct((part, n), F32),
            jax.ShapeDtypeStruct((blocks + away + extra, BLOCK, q), F32),
            jax.ShapeDtypeStruct(parent.shape, F32),
            jax.ShapeDtypeStruct((1,), jnp.int32),
        ),
        in_specs=[SMEM] + [pl.BlockSpec(memory_space=pltpu.HBM)] * 4,
        out_specs=(VMEM,) * 4 + (SMEM,),
        scratch_shapes=[
            pltpu.VMEM((n, n), F32),
            pltpu.VMEM((n // BLOCK, BLOCK, BLOCK), F32),
            pltpu.VMEM((q // grain, grain, n), F32),
            pltpu.VMEM((q // grain, grain, n), F32),
            pltpu.VMEM((q // grain, grain, n), BF16),
            pltpu.VMEM((q // grain, grain, n), BF16),
            pltpu.VMEM((q // grain, grain, n), BF16),
            pltpu.VMEM((q // grain, grain, n), BF16),
            pltpu.VMEM((n, n), BF16),
            pltpu.VMEM((n, n), BF16),
            pltpu.VMEM((n // group, group, group), BF16),
            pltpu.VMEM((n // group, group, group), BF16),
            pltpu.VMEM((blocks, BLOCK, q), F32),
            pltpu.VMEM((away, BLOCK, q), F32),
            pltpu.VMEM((2 * max(extra, 1), BLOCK, q), F32),
            pltpu.VMEM((max(extra, 1), BLOCK, q), F32),
            dma((away,)), dma((away,)),
            dma((2,)), dma((2,)), dma((2,)), dma((2,)),
            dma((4,)), dma((2, 2, columns)), dma((2, columns)), dma((2, columns)), dma((2, columns)),
            dma((2, 2, columns)), dma((2, 2, columns)),
            dma((grains, 2, columns)), dma((grains, columns)),
            dma((grains, 2, columns)), dma((grains, columns)),
        ],
        compiler_params=pltpu.CompilerParams(
            vmem_limit_bytes=40 << 20, collective_id=0, has_side_effects=True
        ),
    )(row_map, *(pltpu.with_memory_space_constraint(x, pltpu.HBM) for x in arrays))


def rest_kernel(owners, sure, more, quarter, map_ref, piece_ref, out_ref, stage, send, recv):
    child, row = lax.axis_index("wide"), lax.axis_index("grow")
    blocks = out_ref.shape[2] // BLOCK
    per_owner = quarter // owners
    barrier = pltpu.get_barrier_semaphore()
    for d in range(1, owners):
        pl.semaphore_signal(
            barrier, inc=1, device_id={"wide": lax.rem(child + d, owners)},
            device_id_type=pl.DeviceIdType.MESH,
        )
    mine = [(map_ref[child, row * blocks + b] % quarter) // per_owner for b in range(blocks)]

    def give_away(s, d):
        return pltpu.make_async_remote_copy(
            src_ref=stage.at[s], dst_ref=out_ref.at[s], send_sem=send.at[s], recv_sem=recv.at[s],
            device_id={"wide": lax.rem(child + d, owners)}, device_id_type=pl.DeviceIdType.MESH,
        )

    slots = [(d, sure + i) for d in range(1, owners) for i in range(more)]
    for s, (d, slot) in enumerate(slots):
        block, rank = jnp.int32(0), jnp.int32(0)
        for b in range(blocks):
            here = mine[b] == lax.rem(child + d, owners)
            block = jnp.where(here & (rank == slot), b, block)
            rank += here.astype(jnp.int32)
        stage[s] = piece_ref[block]
    pl.semaphore_wait(barrier, owners - 1)
    for s, (d, _) in enumerate(slots):
        give_away(s, d).start()
    for s, (d, _) in enumerate(slots):
        give_away(s, d).wait()


def rest_call(row_map, pieces, owners, sure, more, quarter):
    away = (owners - 1) * more
    shape = (away,) + pieces.shape[1:]
    dma = pltpu.SemaphoreType.DMA
    return pl.pallas_call(
        functools.partial(rest_kernel, owners, sure, more, quarter),
        name="rest",
        out_shape=jax.ShapeDtypeStruct(shape, F32),
        in_specs=[SMEM, VMEM],
        out_specs=VMEM,
        scratch_shapes=[pltpu.VMEM(shape, F32), dma((away,)), dma((away,))],
        compiler_params=pltpu.CompilerParams(
            vmem_limit_bytes=12 << 20, collective_id=more, has_side_effects=True
        ),
    )(row_map, pieces)


def add_kernel(owners, sure, more, lend, map_ref, parent_ref, factor_ref, panel_ref, *refs):
    pieces = refs[:-5]
    out_ref, factor_out, panel_out, total, write = refs[-5:]
    per_owner = total.shape[0] // BLOCK
    quarter = owners * per_owner
    q = pieces[0].shape[2]
    blocks = q // BLOCK
    column_blocks = total.shape[1] // BLOCK
    child, row = lax.axis_index("wide"), lax.axis_index("grow")
    column = lax.axis_index("gcol")

    def rows_of(p):
        return pl.ds(pl.multiple_of(p * BLOCK, BLOCK), BLOCK)

    def store(p):
        return pltpu.make_async_copy(total.at[rows_of(p)], out_ref.at[rows_of(p)], write.at[p])

    others = (
        pltpu.make_async_copy(factor_ref, factor_out, write.at[per_owner]),
        pltpu.make_async_copy(panel_ref, panel_out, write.at[per_owner + 1]),
    )

    def add_rows(p, carry):
        total[rows_of(p), :] = parent_ref[rows_of(p), :]

        def add(g, carry):
            block, slot, rank = jnp.int32(-1), jnp.int32(-1), jnp.int32(0)
            for b in range(blocks):
                to = map_ref[g, row * blocks + b] % quarter
                hit = to == child * per_owner + p
                block = jnp.where(hit, b, block)
                slot = jnp.where(hit, rank, slot)
                rank += (to // per_owner == child).astype(jnp.int32)
            away = lax.rem(child - g + owners, owners) - 1

            def put(ref, index):
                for b in range(blocks):
                    to = map_ref[g, column * blocks + b] % column_blocks
                    at = pl.ds(pl.multiple_of(to * BLOCK, BLOCK), BLOCK)
                    total[rows_of(p), at] += ref[index, :, b * BLOCK : b * BLOCK + BLOCK]

            over = slot - sure
            place = blocks + away * sure + slot
            direct = (g == child) | (over < 0)
            if lend:
                beside_row = row + 1 - 2 * lax.rem(row, 2)
                beside = jnp.int32(0)
                for b in range(blocks):
                    to = map_ref[g, beside_row * blocks + b] % quarter
                    beside += (to // per_owner == child).astype(jnp.int32)
                place = blocks + jnp.where(
                    slot == 1, 3, jnp.where((slot == 2) | (slot == 3), slot - 1, slot)
                )
                direct = direct | (beside + over < 4)

            @pl.when((block >= 0) & direct)
            def _():
                put(pieces[0], jnp.where(g == child, block, place))

            if len(pieces) > 1:

                @pl.when((block >= 0) & jnp.logical_not(direct))
                def _():
                    put(pieces[1], away * more + over)

            return carry

        lax.fori_loop(0, owners, add, 0)
        store(p).start()
        return carry

    lax.fori_loop(0, per_owner, add_rows, 0)
    for copy in others:
        copy.start()
    for p in range(per_owner):
        store(p).wait()
    for copy in others:
        copy.wait()


def add_call(row_map, parent, factor, panel, pieces, owners, sure, more, lend):
    dma = pltpu.SemaphoreType.DMA
    per_owner = parent.shape[0] // BLOCK
    anywhere = pl.BlockSpec(memory_space=pl.ANY)
    return pl.pallas_call(
        functools.partial(add_kernel, owners, sure, more, lend),
        name="extend_add",
        out_shape=tuple(jax.ShapeDtypeStruct(x.shape, F32) for x in (parent, factor, panel)),
        in_specs=[SMEM] + [VMEM] * (3 + len(pieces)),
        out_specs=(anywhere,) * 3,
        scratch_shapes=[pltpu.VMEM(parent.shape, F32), dma((per_owner + 2,))],
        compiler_params=pltpu.CompilerParams(vmem_limit_bytes=24 << 20),
    )(row_map, parent, factor, panel, *pieces)


def body(diag_block, lower_block, trailing_block, parent_front, row_map):
    owners = lax.axis_size("wide")
    rows, columns = lax.axis_size("grow"), lax.axis_size("gcol")
    quarter = parent_front.shape[1] * owners // BLOCK
    blocks = trailing_block.shape[1] // BLOCK
    most = most_slots(blocks, quarter // owners)
    sure = max(1, 2 * most // 3)
    lend = lends(owners, sure, most, rows)
    factor, panel, pieces, held, need = front_call(
        row_map, diag_block[0], lower_block[0], trailing_block[0], parent_front[0],
        rows, columns, owners, sure, quarter,
    )

    def finish(more):
        def run():
            extra = (rest_call(row_map, pieces, owners, sure, more, quarter),) if more else ()
            return add_call(
                row_map, held, factor, panel, (pieces,) + extra, owners, sure, more, lend
            )

        return run

    branches = [finish(more) for more in range(most - sure + 1)]
    parent, factor, panel = lax.switch(jnp.clip(need[0] - sure, 0, most - sure), branches)
    return (factor[None], panel[None], parent[None])


def solution(mesh):
    placed = (
        P("wide", ("grow", "gcol"), None),
        P("wide", ("grow", "gcol"), None),
        P("wide", "grow", "gcol"),
        P("grow", "wide", "gcol"),
        P(),
    )
    return jax.shard_map(
        body,
        mesh=mesh,
        in_specs=placed,
        out_specs=(
            P("wide", ("grow", "gcol"), None),
            P("wide", ("grow", "gcol"), None),
            P("grow", "wide", "gcol"),
        ),
        check_vma=False,
    )
```
